32 devices in a mesh: rep: 8 (over z, y), shard: 4 (over x, core).
Axes of the slice: x: 2, y: 2, z: 4, core: 2. Of those that a mesh axis runs over, the one named last changes fastest.
Arguments:
- tokens: bfloat16 [4096, 1024], P(('rep', 'shard')), may hold values from -6 to 6
- segments: int32 [32, 128], P(('rep', 'shard')), may hold values from 0 to 1, never falling along the last dimension, each value on 1 to 96 neighbouring positions
- out_cot: bfloat16 [4096, 1024], P(('rep', 'shard')), may hold values from -6 to 6
- step_count: int32 [1], replicated, may hold values from 1 to 8
- w_qkv: float32 [1024, 4096], P(('rep', 'shard')), may hold values from -0.1875 to 0.1875
- w_out: float32 [2048, 1024], P(('rep', 'shard')), may hold values from -0.5 to 0.5
- w_gate_up: float32 [1024, 6144], P(('rep', 'shard')), may hold values from -0.1875 to 0.1875
- w_down: float32 [3072, 1024], P(('rep', 'shard')), may hold values from -0.109375 to 0.109375
- norm_gains: float32 [2304], P(('rep', 'shard')), may hold values from 0.5 to 1.5
- mean_qkv: float32 [1024, 4096], P(('rep', 'shard')), may hold values from -0.0625 to 0.0625
- mean_out: float32 [2048, 1024], P(('rep', 'shard')), may hold values from -0.0625 to 0.0625
- mean_gate_up: float32 [1024, 6144], P(('rep', 'shard')), may hold values from -0.0625 to 0.0625
- mean_down: float32 [3072, 1024], P(('rep', 'shard')), may hold values from -0.0625 to 0.0625
- mean_gains: float32 [2304], P(('rep', 'shard')), may hold values from -0.0625 to 0.0625
- square_qkv: float32 [1024, 4096], P(('rep', 'shard')), may hold values from 2.4414062e-06 to 0.00024414062
- square_out: float32 [2048, 1024], P(('rep', 'shard')), may hold values from 2.4414062e-06 to 0.00024414062
- square_gate_up: float32 [1024, 6144], P(('rep', 'shard')), may hold values from 2.4414062e-06 to 0.00024414062
- square_down: float32 [3072, 1024], P(('rep', 'shard')), may hold values from 2.4414062e-06 to 0.00024414062
- square_gains: float32 [2304], P(('rep', 'shard')), may hold values from 2.4414062e-06 to 0.00024414062
Outputs:
- layer_out: bfloat16 [4096, 1024], P(('rep', 'shard'))
- input_grad: float32 [4096, 1024], P(('rep', 'shard'))
- grad_qkv: float32 [1024, 4096], P(('rep', 'shard'))
- grad_out: float32 [2048, 1024], P(('rep', 'shard'))
- grad_gate_up: float32 [1024, 6144], P(('rep', 'shard'))
- grad_down: float32 [3072, 1024], P(('rep', 'shard'))
- grad_gains: float32 [2304], P(('rep', 'shard'))
- new_qkv: float32 [1024, 4096], P(('rep', 'shard'))
- new_out: float32 [2048, 1024], P(('rep', 'shard'))
- new_gate_up: float32 [1024, 6144], P(('rep', 'shard'))
- new_down: float32 [3072, 1024], P(('rep', 'shard'))
- new_gains: float32 [2304], P(('rep', 'shard'))
- new_mean_qkv: float32 [1024, 4096], P(('rep', 'shard'))
- new_mean_out: float32 [2048, 1024], P(('rep', 'shard'))
- new_mean_gate_up: float32 [1024, 6144], P(('rep', 'shard'))
- new_mean_down: float32 [3072, 1024], P(('rep', 'shard'))
- new_mean_gains: float32 [2304], P(('rep', 'shard'))
- new_square_qkv: float32 [1024, 4096], P(('rep', 'shard'))
- new_square_out: float32 [2048, 1024], P(('rep', 'shard'))
- new_square_gate_up: float32 [1024, 6144], P(('rep', 'shard'))
- new_square_down: float32 [3072, 1024], P(('rep', 'shard'))
- new_square_gains: float32 [2304], P(('rep', 'shard'))
The draws below stay inside these ranges and needn't reach their ends.
Inputs may be any that keep to these rules, and one draw needn't show every extreme that they name: `segments`: segment ids never fall along a row, and each row's longest document has at most 96 positions.
All inputs are finite; a program needn't handle non-finite values.
Results may differ from the reference program's by a relative error of at most 0.013.
The reference program's roundings to bfloat16 on the way count: a program that leaves them out, or rounds other values in their place, can miss the bound.
Values may be sent and summed in bfloat16 or wider, within the bound.
No kernel may reach another device: no remote copies, remote signals or barrier semaphores. Data moves between devices by JAX's collectives and lax.ppermute only.
A program may use at most 256 MiB of HBM per device.

```python
import math
import jax
import jax.numpy as jnp
import numpy as np
from jax import lax

D = 1024
QUERY_HEADS = 16
KEY_VALUE_HEADS = 8
HEAD_SIZE = 128
FF = 3072
TOK_DEV = 128
SEG_MOST = 96
TOKENS = 4096
ROWS = 32
QKV = 4096
GAINS = 2304
N_REP = 8
N_SHARD = 4


def level_of(key, dims, pieces, low, high):
    factor_of, own = 1.0, jax.random.fold_in(key, 6)
    for dim, blocks in pieces:
        steps = jnp.exp(jax.random.uniform(jax.random.fold_in(own, dim), (blocks,), jnp.float32, low / len(pieces), high / len(pieces)))
        factor_of = factor_of * jnp.repeat(steps, dims[dim] // blocks).reshape([-1 if axis == dim else 1 for axis in range(len(dims))])
    return factor_of


def profile(number_of, total, bound, slope):
    portions = [(1 << 20) // math.isqrt(standing ** slope) + 1 for standing in range(2, number_of + 1)]
    rest, holding = total - bound - (number_of - 1), [1] * (number_of - 1)
    while rest > 0:
        candidates = [i for i in range(number_of - 1) if holding[i] < bound]
        mass, left = sum([portions[i] for i in candidates]), rest
        for i in candidates:
            more = min(bound - holding[i], max(1, left * portions[i] // mass), rest)
            holding[i] = holding[i] + more
            rest = rest - more
    return np.array([bound] + holding)


def uneven(stream_key, amount, total, most, skew):
    if amount == 2:
        one = jax.random.randint(stream_key, (), max(1, total - most), min(most, total - 1) + 1)
        return jnp.stack([one, total - one])
    tallies = jnp.asarray(profile(amount, total, most, skew), jnp.int32)
    couples = (amount - 1) // 2
    source_of, receiver = tallies[1:1 + 2 * couples:2], tallies[2:2 + 2 * couples:2]
    room = jnp.minimum(source_of - 1, most - receiver)
    shifted = jax.random.randint(jax.random.fold_in(stream_key, 1), (couples,), 0, 1 << 20) % (room + 1)
    tallies = tallies.at[1:1 + 2 * couples:2].set(source_of - shifted).at[2:2 + 2 * couples:2].set(receiver + shifted)
    return tallies[jax.random.permutation(jax.random.fold_in(stream_key, 2), amount)]


def centred(own_key, dims, spread, most, pieces=(), held_as=jnp.bfloat16):
    array = spread * jax.random.normal(own_key, dims, jnp.float32)
    if pieces:
        array = array * level_of(own_key, dims, pieces, -0.22, 0.18)
    return jnp.clip(array, -most, most).astype(held_as)


def setup_inputs(seed: int = 0) -> dict:
    arg_keys = jax.random.split(jax.random.key(seed), 20)
    tokens = centred(arg_keys[0], (TOKENS, D), 1.0, 6.0, ((0, 32),))
    segments = jax.vmap(lambda own: jnp.searchsorted(jnp.cumsum(uneven(own, 2, TOK_DEV, SEG_MOST, 0)), jnp.arange(TOK_DEV), side="right"))(jax.random.split(arg_keys[1], ROWS)).reshape((ROWS, TOK_DEV)).astype(jnp.int32)
    out_cot = centred(arg_keys[2], (TOKENS, D), 1.0, 6.0, ((0, 32),))
    step_count = jax.random.randint(arg_keys[3], (1,), 1, 9).astype(jnp.int32)
    w_qkv = centred(arg_keys[4], (D, QKV), D ** -0.5, 0.1875, ((0, 32),), jnp.float32)
    w_out = centred(arg_keys[5], (QUERY_HEADS * HEAD_SIZE, D), (QUERY_HEADS * HEAD_SIZE // 16) ** -0.5, 0.5, ((0, 32),), jnp.float32)
    w_gate_up = centred(arg_keys[6], (D, 2 * FF), D ** -0.5, 0.1875, ((0, 32),), jnp.float32)
    w_down = centred(arg_keys[7], (FF, D), FF ** -0.5, 0.109375, ((0, 32),), jnp.float32)
    norm_gains = jnp.clip(1.0 + 0.1 * jax.random.normal(arg_keys[8], (GAINS,), jnp.float32), 0.5, 1.5)
    mean_qkv = centred(arg_keys[9], (D, QKV), (0.3 * TOKENS ** -0.5), 0.0625, ((0, 32),), jnp.float32)
    mean_out = centred(arg_keys[10], (QUERY_HEADS * HEAD_SIZE, D), (0.3 * TOKENS ** -0.5), 0.0625, ((0, 32),), jnp.float32)
    mean_gate_up = centred(arg_keys[11], (D, 2 * FF), (0.3 * TOKENS ** -0.5), 0.0625, ((0, 32),), jnp.float32)
    mean_down = centred(arg_keys[12], (FF, D), (0.3 * TOKENS ** -0.5), 0.0625, ((0, 32),), jnp.float32)
    mean_gains = centred(arg_keys[13], (GAINS,), (0.3 * TOKENS ** -0.5), 0.0625, ((0, 32),), jnp.float32)
    square_qkv = jnp.clip(jnp.exp(math.log(0.00024414062) - 4.6051702 * jax.random.uniform(arg_keys[14], (D, QKV), jnp.float32) ** level_of(arg_keys[14], (D, QKV), ((0, 32),), -0.2, 0.2)), 2.441406195430318e-06, 0.00024414062)
    square_out = jnp.clip(jnp.exp(math.log(0.00024414062) - 4.6051702 * jax.random.uniform(arg_keys[15], (QUERY_HEADS * HEAD_SIZE, D), jnp.float32) ** level_of(arg_keys[15], (QUERY_HEADS * HEAD_SIZE, D), ((0, 32),), -0.2, 0.2)), 2.441406195430318e-06, 0.00024414062)
    square_gate_up = jnp.clip(jnp.exp(math.log(0.00024414062) - 4.6051702 * jax.random.uniform(arg_keys[16], (D, 2 * FF), jnp.float32) ** level_of(arg_keys[16], (D, 2 * FF), ((0, 32),), -0.2, 0.2)), 2.441406195430318e-06, 0.00024414062)
    square_down = jnp.clip(jnp.exp(math.log(0.00024414062) - 4.6051702 * jax.random.uniform(arg_keys[17], (FF, D), jnp.float32) ** level_of(arg_keys[17], (FF, D), ((0, 32),), -0.2, 0.2)), 2.441406195430318e-06, 0.00024414062)
    square_gains = jnp.clip(jnp.exp(math.log(0.00024414062) - 4.6051702 * jax.random.uniform(arg_keys[18], (GAINS,), jnp.float32) ** level_of(arg_keys[18], (GAINS,), ((0, 32),), -0.2, 0.2)), 2.441406195430318e-06, 0.00024414062)
    return dict(tokens=tokens, segments=segments, out_cot=out_cot, step_count=step_count, w_qkv=w_qkv, w_out=w_out, w_gate_up=w_gate_up, w_down=w_down, norm_gains=norm_gains, mean_qkv=mean_qkv, mean_out=mean_out, mean_gate_up=mean_gate_up, mean_down=mean_down, mean_gains=mean_gains, square_qkv=square_qkv, square_out=square_out, square_gate_up=square_gate_up, square_down=square_down, square_gains=square_gains)


NORM_EPS = 1e-06
ROPE_BASE = 1000000.0
LEARN_RATE = 0.02
BETA_ONE = 0.9
BETA_TWO = 0.95
ADAM_EPS = 1e-08
DECAY_RATE = 0.1

def batched(pattern, left, right):
    return jnp.einsum(pattern, left.astype(jnp.float32), right.astype(jnp.float32))

def rms_forward(signal, gain):
    inverse = lax.rsqrt(lax.optimization_barrier(jnp.mean(signal * signal, axis=-1, keepdims=True)) + NORM_EPS)
    return (signal * inverse * gain, inverse)

def rms_backward(signal, inverse, gain, upstream):
    scaled = upstream * gain
    inner = lax.optimization_barrier(jnp.mean(scaled * signal, axis=-1, keepdims=True))
    d_signal = inverse * (scaled - signal * inverse * inverse * inner)
    d_gain = lax.optimization_barrier(jnp.sum((upstream * signal * inverse).reshape(-1, signal.shape[-1]), axis=0))
    return (d_signal, d_gain)

def rope_tables(length_per_row, width):
    positions = jnp.arange(length_per_row).astype(jnp.float32)
    freqs = jnp.exp(-math.log(ROPE_BASE) * 2.0 * jnp.arange(width // 2).astype(jnp.float32) / width)
    angles = positions[:, None] * freqs[None, :]
    return (jnp.cos(angles)[:, None, :], jnp.sin(angles)[:, None, :])

def apply_rotation(signal, cosine_table, sine_table):
    half_width = signal.shape[-1] // 2
    front_half = signal[..., :half_width]
    back_half = signal[..., half_width:]
    return jnp.concatenate([front_half * cosine_table - back_half * sine_table, back_half * cosine_table + front_half * sine_table], axis=-1)

def unrotate(upstream, cosine_table, sine_table):
    half_width = upstream.shape[-1] // 2
    front_half = upstream[..., :half_width]
    back_half = upstream[..., half_width:]
    return jnp.concatenate([front_half * cosine_table + back_half * sine_table, back_half * cosine_table - front_half * sine_table], axis=-1)

def attention_mask(segment_rows):
    length_per_row = segment_rows.shape[1]
    rows_idx = jnp.arange(length_per_row)[:, None]
    cols_idx = jnp.arange(length_per_row)[None, :]
    causal = (cols_idx <= rows_idx)[None, :, :]
    return causal & (segment_rows[:, :, None] == segment_rows[:, None, :])

def scores_of(rotated_query, k_rot, allowed):
    scores = batched('rikgd,rjkd->rkgij', rotated_query, k_rot)
    return jnp.where(allowed[:, None, None, :, :], scores, -1e+30)

def forward_pass(tokens_rows, segment_rows, qkv_bf, output_half, gate_up_bf, down_bf, gain_all):
    total_rows = tokens_rows.shape[0]
    length_per_row = tokens_rows.shape[1]
    flat = total_rows * length_per_row
    head_group = QUERY_HEADS // KEY_VALUE_HEADS
    query_width = QUERY_HEADS * HEAD_SIZE
    key_width = KEY_VALUE_HEADS * HEAD_SIZE
    x_float = tokens_rows.astype(jnp.float32)
    normed_float, inv_attn = rms_forward(x_float, gain_all[:D])
    normed = normed_float.astype(jnp.bfloat16).reshape(flat, D)
    projected_rows = jnp.dot(normed, qkv_bf, preferred_element_type=jnp.float32).reshape(total_rows, length_per_row, -1)
    queries = projected_rows[..., :query_width].reshape(total_rows, length_per_row, QUERY_HEADS, HEAD_SIZE)
    unnormed_keys = projected_rows[..., query_width:query_width + key_width].reshape(total_rows, length_per_row, KEY_VALUE_HEADS, HEAD_SIZE)
    unnormed_values = projected_rows[..., query_width + key_width:].reshape(total_rows, length_per_row, KEY_VALUE_HEADS, HEAD_SIZE)
    normalized_query, inv_query = rms_forward(queries, gain_all[2 * D:2 * D + HEAD_SIZE])
    key_normed, inv_key = rms_forward(unnormed_keys, gain_all[2 * D + HEAD_SIZE:])
    cosine_table, sine_table = rope_tables(length_per_row, HEAD_SIZE)
    rotated_query = (apply_rotation(normalized_query, cosine_table, sine_table) * (1.0 / math.sqrt(HEAD_SIZE))).astype(jnp.bfloat16).reshape(total_rows, length_per_row, KEY_VALUE_HEADS, head_group, HEAD_SIZE)
    k_rot = apply_rotation(key_normed, cosine_table, sine_table).astype(jnp.bfloat16)
    v_bf = unnormed_values.astype(jnp.bfloat16)
    allowed = attention_mask(segment_rows)
    scores = scores_of(rotated_query, k_rot, allowed)
    peak = lax.optimization_barrier(jnp.max(scores, axis=-1, keepdims=True))
    log_total = peak + jnp.log(lax.optimization_barrier(jnp.sum(jnp.exp(scores - peak), axis=-1, keepdims=True)))
    probs_bf = jnp.exp(scores - log_total).astype(jnp.bfloat16)
    attended = batched('rkgij,rjkd->rikgd', probs_bf, v_bf)
    attended_bf = attended.astype(jnp.bfloat16).reshape(flat, query_width)
    x_mid = x_float + jnp.dot(attended_bf, output_half, preferred_element_type=jnp.float32).reshape(total_rows, length_per_row, D)
    mid_float, inv_mlp = rms_forward(x_mid, gain_all[D:2 * D])
    mid_normed = mid_float.astype(jnp.bfloat16).reshape(flat, D)
    gated = jnp.dot(mid_normed, gate_up_bf, preferred_element_type=jnp.float32)
    gate_pre = gated[:, :FF]
    up_pre = gated[:, FF:]
    hidden = (jax.nn.silu(gate_pre) * up_pre).astype(jnp.bfloat16)
    layer_rows = (x_mid + jnp.dot(hidden, down_bf, preferred_element_type=jnp.float32).reshape(total_rows, length_per_row, D)).astype(jnp.bfloat16)
    saved = {'x_float': x_float, 'inv_attn': inv_attn, 'normed': normed, 'queries': queries, 'keys_raw': unnormed_keys, 'inv_query': inv_query, 'inv_key': inv_key, 'q_rot': rotated_query, 'k_rot': k_rot, 'v_bf': v_bf, 'allowed': allowed, 'log_total': log_total, 'attended': attended, 'attended_bf': attended_bf, 'x_mid': x_mid, 'inv_mlp': inv_mlp, 'mid_normed': mid_normed, 'gate_pre': gate_pre, 'up_pre': up_pre, 'hidden': hidden}
    return (layer_rows, saved)

def ffn_backward(saved, cot_rows, gate_up_bf, down_bf, gain_all):
    total_rows = cot_rows.shape[0]
    length_per_row = cot_rows.shape[1]
    cot_flat = cot_rows.reshape(total_rows * length_per_row, D)
    gate_pre = saved['gate_pre']
    grad_down = jnp.dot(saved['hidden'].T, cot_flat, preferred_element_type=jnp.float32)
    d_hidden = jnp.dot(cot_flat, down_bf.T, preferred_element_type=jnp.float32)
    sig_gate = jax.nn.sigmoid(gate_pre)
    d_gate = d_hidden * saved['up_pre'] * sig_gate * (1.0 + gate_pre * (1.0 - sig_gate))
    d_upper = d_hidden * gate_pre * sig_gate
    d_gated = jnp.concatenate([d_gate, d_upper], axis=1).astype(jnp.bfloat16)
    grad_gate_up = jnp.dot(saved['mid_normed'].T, d_gated, preferred_element_type=jnp.float32)
    d_mid_norm = jnp.dot(d_gated, gate_up_bf.T, preferred_element_type=jnp.float32).reshape(total_rows, length_per_row, D)
    d_mid_part, d_mlp_gain = rms_backward(saved['x_mid'], saved['inv_mlp'], gain_all[D:2 * D], d_mid_norm)
    return (grad_gate_up, grad_down, cot_rows.astype(jnp.float32) + d_mid_part, d_mlp_gain)

def attn_backward(saved, d_mid, qkv_bf, output_half, gain_all):
    total_rows = d_mid.shape[0]
    length_per_row = d_mid.shape[1]
    flat = total_rows * length_per_row
    head_group = QUERY_HEADS // KEY_VALUE_HEADS
    query_width = QUERY_HEADS * HEAD_SIZE
    key_width = KEY_VALUE_HEADS * HEAD_SIZE
    middle_gradient_half = d_mid.astype(jnp.bfloat16).reshape(flat, D)
    grad_out = jnp.dot(saved['attended_bf'].T, middle_gradient_half, preferred_element_type=jnp.float32)
    attention_gradient = jnp.dot(middle_gradient_half, output_half.T, preferred_element_type=jnp.float32).astype(jnp.bfloat16).reshape(total_rows, length_per_row, KEY_VALUE_HEADS, head_group, HEAD_SIZE)
    delta = lax.optimization_barrier(jnp.sum(attention_gradient.astype(jnp.float32) * saved['attended'], axis=-1))
    delta = jnp.transpose(delta, (0, 2, 3, 1))[..., None]
    scores = scores_of(saved['q_rot'], saved['k_rot'], saved['allowed'])
    probs = jnp.exp(scores - saved['log_total'])
    probs_bf = probs.astype(jnp.bfloat16)
    d_probs = batched('rikgd,rjkd->rkgij', attention_gradient, saved['v_bf'])
    d_scores = (probs * (d_probs - delta)).astype(jnp.bfloat16)
    d_values = batched('rkgij,rikgd->rjkd', probs_bf, attention_gradient)
    d_qrot = batched('rkgij,rjkd->rikgd', d_scores, saved['k_rot']).reshape(total_rows, length_per_row, QUERY_HEADS, HEAD_SIZE)
    d_krot = batched('rkgij,rikgd->rjkd', d_scores, saved['q_rot'])
    cosine_table, sine_table = rope_tables(length_per_row, HEAD_SIZE)
    d_queries, d_query_gain = rms_backward(saved['queries'], saved['inv_query'], gain_all[2 * D:2 * D + HEAD_SIZE], unrotate(d_qrot * (1.0 / math.sqrt(HEAD_SIZE)), cosine_table, sine_table))
    d_keys, d_key_gain = rms_backward(saved['keys_raw'], saved['inv_key'], gain_all[2 * D + HEAD_SIZE:], unrotate(d_krot, cosine_table, sine_table))
    d_projected = jnp.concatenate([d_queries.reshape(flat, query_width), d_keys.reshape(flat, key_width), d_values.reshape(flat, key_width)], axis=1).astype(jnp.bfloat16)
    grad_qkv = jnp.dot(saved['normed'].T, d_projected, preferred_element_type=jnp.float32)
    d_normed = jnp.dot(d_projected, qkv_bf.T, preferred_element_type=jnp.float32).reshape(total_rows, length_per_row, D)
    d_input_part, d_attn_gain = rms_backward(saved['x_float'], saved['inv_attn'], gain_all[:D], d_normed)
    return (grad_qkv, grad_out, d_attn_gain, d_query_gain, d_key_gain, d_mid + d_input_part)

def adamw(weight, grad_sum, mean_old, square_old, step_float, token_total, decay):
    gradient = grad_sum / token_total
    mean_new = BETA_ONE * mean_old + (1.0 - BETA_ONE) * gradient
    square_new = BETA_TWO * square_old + (1.0 - BETA_TWO) * gradient * gradient
    fix_one = 1.0 - jnp.power(BETA_ONE, step_float)
    fix_two = 1.0 - jnp.power(BETA_TWO, step_float)
    change = mean_new / fix_one / (jnp.sqrt(square_new / fix_two) + ADAM_EPS) + decay * weight
    return (weight - LEARN_RATE * change, mean_new, square_new)

def reference(tokens, segments, out_cot, step_count, w_qkv, w_out, w_gate_up, w_down, norm_gains, mean_qkv, mean_out, mean_gate_up, mean_down, mean_gains, square_qkv, square_out, square_gate_up, square_down, square_gains):
    row_count = N_REP * N_SHARD
    block_rows = math.gcd(row_count, max(1, 4096 // TOK_DEV))
    block_count = row_count // block_rows
    qkv_bf = w_qkv.astype(jnp.bfloat16)
    output_half = w_out.astype(jnp.bfloat16)
    gate_up_bf = w_gate_up.astype(jnp.bfloat16)
    down_bf = w_down.astype(jnp.bfloat16)
    gain_all = lax.optimization_barrier(norm_gains.astype(jnp.bfloat16)).astype(jnp.float32)
    stacked = (tokens.reshape(block_count, block_rows, TOK_DEV, D), segments.reshape(block_count, block_rows, TOK_DEV), out_cot.reshape(block_count, block_rows, TOK_DEV, D))

    def one_block(carry, items):
        tokens_rows, segment_rows, cot_rows = items
        layer_rows, saved = forward_pass(tokens_rows, segment_rows, qkv_bf, output_half, gate_up_bf, down_bf, gain_all)
        grad_gate_up, grad_down, d_mid, d_mlp_gain = ffn_backward(saved, cot_rows, gate_up_bf, down_bf, gain_all)
        grad_qkv, grad_out, d_attn_gain, d_query_gain, d_key_gain, input_rows = attn_backward(saved, d_mid, qkv_bf, output_half, gain_all)
        grad_gains = jnp.concatenate([d_attn_gain, d_mlp_gain, d_query_gain, d_key_gain])
        totals = (carry[0] + grad_qkv, carry[1] + grad_out, carry[2] + grad_gate_up, carry[3] + grad_down, carry[4] + grad_gains)
        return (totals, (layer_rows, input_rows))
    start = (jnp.zeros(w_qkv.shape, jnp.float32), jnp.zeros(w_out.shape, jnp.float32), jnp.zeros(w_gate_up.shape, jnp.float32), jnp.zeros(w_down.shape, jnp.float32), jnp.zeros(norm_gains.shape, jnp.float32))
    totals, outputs = lax.scan(one_block, start, stacked)
    layer_out = outputs[0].reshape(TOKENS, D)
    input_grad = outputs[1].reshape(TOKENS, D)
    step_float = step_count[0].astype(jnp.float32)
    token_total = float(TOKENS)
    new_qkv, new_mean_qkv, new_square_qkv = adamw(w_qkv, totals[0], mean_qkv, square_qkv, step_float, token_total, DECAY_RATE)
    new_out, new_mean_out, new_square_out = adamw(w_out, totals[1], mean_out, square_out, step_float, token_total, DECAY_RATE)
    new_gate_up, new_mean_gate_up, new_square_gate_up = adamw(w_gate_up, totals[2], mean_gate_up, square_gate_up, step_float, token_total, DECAY_RATE)
    new_down, new_mean_down, new_square_down = adamw(w_down, totals[3], mean_down, square_down, step_float, token_total, DECAY_RATE)
    new_gains, new_mean_gains, new_square_gains = adamw(norm_gains, totals[4], mean_gains, square_gains, step_float, token_total, 0.0)
    return (layer_out, input_grad, totals[0], totals[1], totals[2], totals[3], totals[4], new_qkv, new_out, new_gate_up, new_down, new_gains, new_mean_qkv, new_mean_out, new_mean_gate_up, new_mean_down, new_mean_gains, new_square_qkv, new_square_out, new_square_gate_up, new_square_down, new_square_gains)
```

```python
import math

import jax
import jax.numpy as jnp
from jax import lax
from jax.sharding import PartitionSpec as P

D = 1024
QUERY_HEADS = 16
KEY_VALUE_HEADS = 8
HEAD_SIZE = 128
FF = 3072


NORM_EPS = 1e-06
ROPE_BASE = 1000000.0
LEARN_RATE = 0.02
BETA_ONE = 0.9
BETA_TWO = 0.95
ADAM_EPS = 1e-08
DECAY_RATE = 0.1


def batched(pattern, left, right):
    return jnp.einsum(pattern, left, right, preferred_element_type=jnp.float32)


def rms_forward(signal, gain):
    inverse = lax.rsqrt(jnp.mean(signal * signal, axis=-1, keepdims=True) + NORM_EPS)
    return (signal * inverse * gain, inverse)


def rms_backward(signal, inverse, gain, upstream):
    scaled = upstream * gain
    inner = jnp.mean(scaled * signal, axis=-1, keepdims=True)
    d_signal = inverse * (scaled - signal * inverse * inverse * inner)
    d_gain = jnp.sum((upstream * signal * inverse).reshape(-1, signal.shape[-1]), axis=0)
    return (d_signal, d_gain)


def rope_tables(length_per_row, width):
    positions = jnp.arange(length_per_row).astype(jnp.float32)
    freqs = jnp.exp(-math.log(ROPE_BASE) * 2.0 * jnp.arange(width // 2).astype(jnp.float32) / width)
    angles = positions[:, None] * freqs[None, :]
    return (jnp.cos(angles)[:, None, :], jnp.sin(angles)[:, None, :])


def apply_rotation(signal, cosine_table, sine_table):
    half_width = signal.shape[-1] // 2
    front_half = signal[..., :half_width]
    back_half = signal[..., half_width:]
    return jnp.concatenate(
        [
            front_half * cosine_table - back_half * sine_table,
            back_half * cosine_table + front_half * sine_table,
        ],
        axis=-1,
    )


def unrotate(upstream, cosine_table, sine_table):
    half_width = upstream.shape[-1] // 2
    front_half = upstream[..., :half_width]
    back_half = upstream[..., half_width:]
    return jnp.concatenate(
        [
            front_half * cosine_table + back_half * sine_table,
            back_half * cosine_table - front_half * sine_table,
        ],
        axis=-1,
    )


def attention_mask(segment_rows):
    length_per_row = segment_rows.shape[1]
    rows_idx = jnp.arange(length_per_row)[:, None]
    cols_idx = jnp.arange(length_per_row)[None, :]
    causal = (cols_idx <= rows_idx)[None, :, :]
    return causal & (segment_rows[:, :, None] == segment_rows[:, None, :])


def scores_of(rotated_query, k_rot, allowed):
    scores = batched("rikgd,rjkd->rkgij", rotated_query, k_rot)
    return jnp.where(allowed[:, None, None, :, :], scores, -1e30)


def xor_perm(axis_size, bit):
    return [(i, i ^ bit) for i in range(axis_size)]


def group_gather(part):
    far = lax.ppermute(part, "shard", xor_perm(4, 2))
    pair = jnp.stack([part, far])
    near = lax.ppermute(pair, "shard", xor_perm(4, 1))
    return jnp.stack([part, near[0], far, near[1]])


def group_sum(partial):
    near = lax.ppermute(
        jnp.stack([partial[3], partial[1]]).astype(jnp.bfloat16), "shard", xor_perm(4, 1)
    )
    outgoing = (partial[2] + near[0].astype(jnp.float32)).astype(jnp.bfloat16)
    far = lax.ppermute(outgoing, "shard", xor_perm(4, 2))
    return partial[0] + near[1].astype(jnp.float32) + far.astype(jnp.float32)


def after(value, *earlier):
    return lax.optimization_barrier((value,) + earlier)[0]


RING = [(2 * z + y, 2 * ((z + 1) % 4) + y) for z in range(4) for y in range(2)]


def in_order(blocks, z, rows):
    row = jnp.concatenate([blocks[3], blocks[2], blocks[1], blocks[0], blocks[3], blocks[2], blocks[1]])
    return lax.dynamic_slice_in_dim(row, (3 - z) * rows, 4 * rows, axis=0)


def gather_rep(long, wide, ahead=()):
    if lax.axis_size("rep") != 8:
        return tuple(lax.all_gather(x, "rep", axis=0, tiled=True) for x in (long, wide)) + ((),)
    place = lax.axis_index("rep")
    z, even = place // 2, place % 2 == 0
    rows, columns = long.shape
    width = wide.shape[0]
    longs = [after(long, *ahead[:1])] if ahead else [long]
    wide_in = after(wide, *ahead[:1]) if ahead else wide
    longs.append(lax.ppermute(longs[-1], "rep", RING))
    other = lax.ppermute(wide_in, "rep", xor_perm(8, 1))
    wides = [jnp.where(even, jnp.concatenate([wide, other]), jnp.concatenate([other, wide]))]
    for k in range(3):
        if k:
            longs.append(lax.ppermute(longs[-1], "rep", RING))
        wides.append(lax.ppermute(wides[-1], "rep", RING))
    mine = in_order(longs, z, rows)
    other = lax.ppermute(mine, "rep", xor_perm(8, 1))
    mine, other = mine.reshape(4, rows, columns), other.reshape(4, rows, columns)
    both = jnp.stack([jnp.where(even, mine, other), jnp.where(even, other, mine)], axis=1)
    return both.reshape(8 * rows, columns), in_order(wides, z, 2 * width), (longs[1], longs[2], longs[3])


def as_bf(value):
    return value.astype(jnp.bfloat16)


def ring_sum(held, z):
    def entry(back):
        return lax.dynamic_index_in_dim(held, (z + 4 - back) % 4, axis=0, keepdims=False)

    got = lax.ppermute(as_bf(entry(1)), "rep", RING)
    for back in (2, 3):
        got = lax.ppermute(as_bf(entry(back) + got.astype(jnp.float32)), "rep", RING)
    return entry(0) + got.astype(jnp.float32)


def sum_pair_first(partial):
    if lax.axis_size("rep") != 8:
        return lax.psum_scatter(partial, "rep", scatter_dimension=0, tiled=True)
    rows, columns = partial.shape[0] // 8, partial.shape[1]
    place = lax.axis_index("rep")
    z, y = place // 2, place % 2
    blocks = partial.reshape(4, 2, rows, columns)
    outgoing = lax.dynamic_index_in_dim(blocks, 1 - y, axis=1, keepdims=False)
    kept = lax.dynamic_index_in_dim(blocks, y, axis=1, keepdims=False)
    got = lax.ppermute(as_bf(outgoing), "rep", xor_perm(8, 1))
    return ring_sum(kept + got.astype(jnp.float32), z)


def sum_ring_first(partial):
    if lax.axis_size("rep") != 8:
        return lax.psum_scatter(partial, "rep", scatter_dimension=0, tiled=True)
    rows, columns = partial.shape[0] // 8, partial.shape[1]
    place = lax.axis_index("rep")
    z, y = place // 2, place % 2
    pair = ring_sum(partial.reshape(4, 2, rows, columns), z)
    outgoing = lax.dynamic_index_in_dim(pair, 1 - y, axis=0, keepdims=False)
    kept = lax.dynamic_index_in_dim(pair, y, axis=0, keepdims=False)
    return kept + lax.ppermute(as_bf(outgoing), "rep", xor_perm(8, 1)).astype(jnp.float32)


def columns_of(array, widths, index):
    start, parts = 0, []
    for width in widths:
        parts.append(
            lax.dynamic_slice_in_dim(array, start + index * (width // 4), width // 4, axis=1)
        )
        start += width
    return jnp.concatenate(parts, axis=1)


def trade(pieces, mine):
    far = lax.ppermute(jnp.stack([pieces(2), pieces(3)]), "shard", xor_perm(4, 2))
    near = lax.ppermute(jnp.stack([pieces(1), far[1]]), "shard", xor_perm(4, 1))
    return [pieces(0), near[0], far[0], near[1]]


def split_columns(array, widths):
    rows = array.shape[0]
    mine = lax.axis_index("shard")
    result = jnp.zeros((4 * rows, sum(widths) // 4), array.dtype)
    for k, piece in enumerate(trade(lambda k: columns_of(array, widths, mine ^ k), mine)):
        result = lax.dynamic_update_slice_in_dim(result, piece, (mine ^ k) * rows, axis=0)
    return result


def join_columns(array, widths):
    rows = array.shape[0] // 4
    mine = lax.axis_index("shard")
    result = jnp.zeros((rows, sum(widths)), jnp.float32)
    own = lax.dynamic_slice_in_dim(array, mine * rows, rows, axis=0)
    array = as_bf(array)
    got = trade(lambda k: lax.dynamic_slice_in_dim(array, (mine ^ k) * rows, rows, axis=0), mine)
    for k, piece in enumerate([own] + got[1:]):
        piece = piece.astype(jnp.float32)
        start, taken = 0, 0
        for width in widths:
            result = lax.dynamic_update_slice(
                result,
                piece[:, taken : taken + width // 4],
                (0, start + (mine ^ k) * (width // 4)),
            )
            start += width
            taken += width // 4
    return result


def turned(inverse):
    rep, shard = lax.axis_size("rep"), lax.axis_size("shard")
    pairs = [(b, (b % rep) * shard + b // rep) for b in range(rep * shard)]
    return [(b, a) for a, b in pairs] if inverse else pairs


def by_shard(parts, mine):
    swapped = jnp.where(mine % 2 == 0, parts, parts[jnp.array([1, 0, 3, 2])])
    return jnp.where(mine // 2 == 0, swapped, jnp.concatenate([swapped[2:], swapped[:2]]))


def sum_gains(partial):
    rep = lax.axis_size("rep")
    if rep != 8:
        return lax.psum(partial, ("rep", "shard"))
    for axis, size, bit in (("shard", 4, 1), ("shard", 4, 2), ("rep", 8, 1), ("rep", 8, 2), ("rep", 8, 4)):
        partial = partial + lax.ppermute(partial, axis, xor_perm(size, bit))
    return partial


QKV_WIDTHS = (QUERY_HEADS * HEAD_SIZE, KEY_VALUE_HEADS * HEAD_SIZE, KEY_VALUE_HEADS * HEAD_SIZE)
GATE_UP_WIDTHS = (FF, FF)


def dot(left, right):
    return jnp.dot(left, right, preferred_element_type=jnp.float32)


def attention_forward(projected, segment_rows, query_gain, key_gain):
    total_rows, length = segment_rows.shape
    heads, kv_heads = QUERY_HEADS // 4, KEY_VALUE_HEADS // 4
    group = heads // kv_heads
    wide, narrow = heads * HEAD_SIZE, kv_heads * HEAD_SIZE
    rows = projected.reshape(total_rows, length, -1)
    queries = rows[..., :wide].reshape(total_rows, length, heads, HEAD_SIZE)
    keys = rows[..., wide : wide + narrow].reshape(total_rows, length, kv_heads, HEAD_SIZE)
    values = rows[..., wide + narrow :].reshape(total_rows, length, kv_heads, HEAD_SIZE)
    normalized, inv_query = rms_forward(queries, query_gain)
    key_normed, inv_key = rms_forward(keys, key_gain)
    cosine, sine = rope_tables(length, HEAD_SIZE)
    q_rot = (
        (apply_rotation(normalized, cosine, sine) * (1.0 / math.sqrt(HEAD_SIZE)))
        .astype(jnp.bfloat16)
        .reshape(total_rows, length, kv_heads, group, HEAD_SIZE)
    )
    k_rot = apply_rotation(key_normed, cosine, sine).astype(jnp.bfloat16)
    v_bf = values.astype(jnp.bfloat16)
    scores = scores_of(q_rot, k_rot, attention_mask(segment_rows))
    peak = jnp.max(scores, axis=-1, keepdims=True)
    log_total = peak + jnp.log(jnp.sum(jnp.exp(scores - peak), axis=-1, keepdims=True))
    probs = jnp.exp(scores - log_total)
    attended = batched("rkgij,rjkd->rikgd", probs.astype(jnp.bfloat16), v_bf)
    saved = (queries, keys, inv_query, inv_key, q_rot, k_rot, v_bf, probs, attended)
    return attended.astype(jnp.bfloat16).reshape(total_rows * length, wide), saved


def attention_backward(saved, d_att, query_gain, key_gain):
    queries, keys, inv_query, inv_key, q_rot, k_rot, v_bf, probs, attended = saved
    total_rows, length = q_rot.shape[:2]
    d_att = d_att.reshape(q_rot.shape)
    delta = jnp.sum(d_att.astype(jnp.float32) * attended, axis=-1)
    delta = jnp.transpose(delta, (0, 2, 3, 1))[..., None]
    d_probs = batched("rikgd,rjkd->rkgij", d_att, v_bf)
    d_scores = (probs * (d_probs - delta)).astype(jnp.bfloat16)
    d_values = batched("rkgij,rikgd->rjkd", probs.astype(jnp.bfloat16), d_att)
    d_qrot = batched("rkgij,rjkd->rikgd", d_scores, k_rot).reshape(queries.shape)
    d_krot = batched("rkgij,rikgd->rjkd", d_scores, q_rot)
    cosine, sine = rope_tables(length, HEAD_SIZE)
    d_queries, d_query_gain = rms_backward(
        queries, inv_query, query_gain, unrotate(d_qrot * (1.0 / math.sqrt(HEAD_SIZE)), cosine, sine)
    )
    d_keys, d_key_gain = rms_backward(keys, inv_key, key_gain, unrotate(d_krot, cosine, sine))
    flat = total_rows * length
    d_projected = jnp.concatenate(
        [d_queries.reshape(flat, -1), d_keys.reshape(flat, -1), d_values.reshape(flat, -1)], axis=1
    ).astype(jnp.bfloat16)
    return d_projected, d_query_gain, d_key_gain


def adamw(weight, grad_sum, mean_old, square_old, step_float, token_total, decay):
    gradient = grad_sum / token_total
    mean_new = BETA_ONE * mean_old + (1.0 - BETA_ONE) * gradient
    square_new = BETA_TWO * square_old + (1.0 - BETA_TWO) * gradient * gradient
    fix_one = 1.0 - jnp.power(BETA_ONE, step_float)
    fix_two = 1.0 - jnp.power(BETA_TWO, step_float)
    change = mean_new / fix_one / (jnp.sqrt(square_new / fix_two) + ADAM_EPS) + decay * weight
    return (weight - LEARN_RATE * change, mean_new, square_new)


def body(
    tokens,
    segments,
    out_cot,
    step_count,
    w_qkv,
    w_out,
    w_gate_up,
    w_down,
    norm_gains,
    mean_qkv,
    mean_out,
    mean_gate_up,
    mean_down,
    mean_gains,
    square_qkv,
    square_out,
    square_gate_up,
    square_down,
    square_gains,
):
    length = tokens.shape[0]
    bf = jnp.bfloat16
    both = ("rep", "shard")
    mine = lax.axis_index("shard")
    own = norm_gains.shape[0]
    extra = jnp.zeros((16, D), bf)
    extra = lax.dynamic_update_slice(extra, norm_gains.astype(bf)[None], (0, 0))
    extra = lax.dynamic_update_slice(extra, segments.astype(bf), (1, 0))
    group = group_gather(jnp.concatenate([tokens, extra]))
    token_group = group[:, :length].reshape(4 * length, D)
    segment_group = group[:, length + 1, :length]
    gain_row = by_shard(group[:, length, :own], mine).reshape(1, 4 * own)
    split = split_columns(
        jnp.concatenate([w_qkv, w_gate_up], axis=1).astype(bf), QKV_WIDTHS + GATE_UP_WIDTHS
    )
    narrow = sum(QKV_WIDTHS) // 4
    block = jnp.concatenate([split[:, :narrow], jnp.zeros((16, narrow), bf)])
    block = lax.dynamic_update_slice(block, gain_row, (4 * w_qkv.shape[0], 0))
    turn = lax.ppermute(jnp.concatenate([w_out, w_down]).astype(bf), both, turned(False))
    qkv, output, steps = gather_rep(block, turn[: w_out.shape[0]])
    gate_up, down, _ = gather_rep(split[:, narrow:], turn[w_out.shape[0] :], steps)
    qkv = qkv.reshape(-1, 4 * w_qkv.shape[0] + 16, narrow)
    gains = qkv[:, 4 * w_qkv.shape[0], : 4 * own].reshape(-1).astype(jnp.float32)
    qkv = qkv[:, : 4 * w_qkv.shape[0]].reshape(D, narrow)
    cot_group = group_gather(after(out_cot, steps[0]) if steps else out_cot).reshape(4 * length, D)
    attn_gain, mlp_gain = gains[:D], gains[D : 2 * D]
    query_gain, key_gain = gains[2 * D : 2 * D + HEAD_SIZE], gains[2 * D + HEAD_SIZE :]

    x_float = tokens.astype(jnp.float32)
    normed = rms_forward(token_group.astype(jnp.float32), attn_gain)[0].astype(bf)
    inv_attn = rms_forward(x_float, attn_gain)[1]
    attended_bf, saved = attention_forward(dot(normed, qkv), segment_group, query_gain, key_gain)
    x_mid = x_float + group_sum(dot(attended_bf, output).reshape(4, length, D))
    mid_float, inv_mlp = rms_forward(x_mid, mlp_gain)
    mid_normed = group_gather(mid_float.astype(bf)).reshape(4 * length, D)
    gated = dot(mid_normed, gate_up)
    half = gated.shape[1] // 2
    gate_pre, up_pre = gated[:, :half], gated[:, half:]
    hidden = (jax.nn.silu(gate_pre) * up_pre).astype(bf)
    layer_out = (x_mid + group_sum(dot(hidden, down).reshape(4, length, D))).astype(bf)

    sum_down = lax.ppermute(
        sum_ring_first(dot(hidden.T, cot_group)).astype(bf), both, turned(True)
    ).astype(jnp.float32)
    d_hidden = dot(cot_group, down.T)
    sig = jax.nn.sigmoid(gate_pre)
    d_gated = jnp.concatenate(
        [d_hidden * up_pre * sig * (1.0 + gate_pre * (1.0 - sig)), d_hidden * gate_pre * sig], axis=1
    ).astype(bf)
    d_mid_norm = group_sum(dot(d_gated, gate_up.T).reshape(4, length, D))
    d_mid_part, d_mlp_gain = rms_backward(x_mid, inv_mlp, mlp_gain, d_mid_norm)
    d_mid = out_cot.astype(jnp.float32) + d_mid_part
    sum_gate_up = join_columns(sum_pair_first(dot(mid_normed.T, d_gated)), GATE_UP_WIDTHS)
    d_mid_bf = group_gather(d_mid.astype(bf)).reshape(4 * length, D)
    sum_out = lax.ppermute(
        sum_pair_first(dot(attended_bf.T, d_mid_bf)).astype(bf), both, turned(True)
    ).astype(jnp.float32)
    d_att = dot(d_mid_bf, output.T).astype(bf)
    d_projected, d_query_gain, d_key_gain = attention_backward(saved, d_att, query_gain, key_gain)
    cut = d_projected.shape[1] // 2
    grad_qkv = dot(normed.T, d_projected)
    sum_qkv = join_columns(
        jnp.concatenate([sum_pair_first(grad_qkv[:, :cut]), sum_ring_first(grad_qkv[:, cut:])], axis=1),
        QKV_WIDTHS,
    )
    d_normed = group_sum(dot(d_projected, qkv.T).reshape(4, length, D))
    d_input_part, d_attn_gain = rms_backward(x_float, inv_attn, attn_gain, d_normed)
    input_grad = d_mid + d_input_part
    gain_grads = sum_gains(
        jnp.concatenate([d_attn_gain, d_mlp_gain, d_query_gain, d_key_gain]).reshape(-1, 128)
    ).reshape(-1)
    place = lax.axis_index("rep") * 4 + lax.axis_index("shard")
    sum_gain = lax.dynamic_slice_in_dim(gain_grads, place * own, own)

    token_total = float(length * lax.axis_size(both))
    step_float = step_count[0].astype(jnp.float32)
    new_qkv, new_mean_qkv, new_square_qkv = adamw(
        w_qkv, sum_qkv, mean_qkv, square_qkv, step_float, token_total, DECAY_RATE
    )
    new_out, new_mean_out, new_square_out = adamw(
        w_out, sum_out, mean_out, square_out, step_float, token_total, DECAY_RATE
    )
    new_gate_up, new_mean_gate_up, new_square_gate_up = adamw(
        w_gate_up, sum_gate_up, mean_gate_up, square_gate_up, step_float, token_total, DECAY_RATE
    )
    new_down, new_mean_down, new_square_down = adamw(
        w_down, sum_down, mean_down, square_down, step_float, token_total, DECAY_RATE
    )
    new_gains, new_mean_gains, new_square_gains = adamw(
        norm_gains, sum_gain, mean_gains, square_gains, step_float, token_total, 0.0
    )
    return (
        layer_out,
        input_grad,
        sum_qkv,
        sum_out,
        sum_gate_up,
        sum_down,
        sum_gain,
        new_qkv,
        new_out,
        new_gate_up,
        new_down,
        new_gains,
        new_mean_qkv,
        new_mean_out,
        new_mean_gate_up,
        new_mean_down,
        new_mean_gains,
        new_square_qkv,
        new_square_out,
        new_square_gate_up,
        new_square_down,
        new_square_gains,
    )


def solution(mesh):
    return jax.shard_map(
        body,
        mesh=mesh,
        in_specs=(
            P(("rep", "shard"), None),
            P(("rep", "shard"), None),
            P(("rep", "shard"), None),
            P(),
            P(("rep", "shard"), None),
            P(("rep", "shard"), None),
            P(("rep", "shard"), None),
            P(("rep", "shard"), None),
            P(("rep", "shard")),
            P(("rep", "shard"), None),
            P(("rep", "shard"), None),
            P(("rep", "shard"), None),
            P(("rep", "shard"), None),
            P(("rep", "shard")),
            P(("rep", "shard"), None),
            P(("rep", "shard"), None),
            P(("rep", "shard"), None),
            P(("rep", "shard"), None),
            P(("rep", "shard")),
        ),
        out_specs=(
            P(("rep", "shard"), None),
            P(("rep", "shard"), None),
            P(("rep", "shard"), None),
            P(("rep", "shard"), None),
            P(("rep", "shard"), None),
            P(("rep", "shard"), None),
            P(("rep", "shard")),
            P(("rep", "shard"), None),
            P(("rep", "shard"), None),
            P(("rep", "shard"), None),
            P(("rep", "shard"), None),
            P(("rep", "shard")),
            P(("rep", "shard"), None),
            P(("rep", "shard"), None),
            P(("rep", "shard"), None),
            P(("rep", "shard"), None),
            P(("rep", "shard")),
            P(("rep", "shard"), None),
            P(("rep", "shard"), None),
            P(("rep", "shard"), None),
            P(("rep", "shard"), None),
            P(("rep", "shard")),
        ),
        check_vma=False,
    )
```

```python
import math

import jax
import jax.numpy as jnp
import numpy as np
from jax import lax
from jax.experimental import pallas as pl
from jax.experimental.pallas import tpu as pltpu
from jax.sharding import PartitionSpec as P

D = 1024
QUERY_HEADS = 16
KEY_VALUE_HEADS = 8
HEAD_SIZE = 128
FF = 3072


NORM_EPS = 1e-06
ROPE_BASE = 1000000.0
LEARN_RATE = 0.02
BETA_ONE = 0.9
BETA_TWO = 0.95
ADAM_EPS = 1e-08
DECAY_RATE = 0.1


def rms_forward(signal, gain):
    inverse = lax.rsqrt(jnp.mean(signal * signal, axis=-1, keepdims=True) + NORM_EPS)
    return (signal * inverse * gain, inverse)


def rms_backward(signal, inverse, gain, upstream):
    scaled = upstream * gain
    inner = jnp.mean(scaled * signal, axis=-1, keepdims=True)
    d_signal = inverse * (scaled - signal * inverse * inverse * inner)
    d_gain = jnp.sum((upstream * signal * inverse).reshape(-1, signal.shape[-1]), axis=0)
    return (d_signal, d_gain)


def xor_perm(axis_size, bit):
    return [(i, i ^ bit) for i in range(axis_size)]


def group_gather(part):
    near = lax.ppermute(part, "shard", xor_perm(4, 1))
    far = lax.ppermute(part, "shard", xor_perm(4, 2))
    return part, near, far, lax.ppermute(far, "shard", xor_perm(4, 1))


def group_sum(send, keep):
    near = lax.ppermute(send, "shard", xor_perm(4, 1))
    far = lax.ppermute(as_bf(keep[1] + near[0].astype(jnp.float32)), "shard", xor_perm(4, 2))
    return keep[0] + near[1].astype(jnp.float32) + far.astype(jnp.float32)


def after(value, *earlier):
    if not earlier:
        return value
    return lax.optimization_barrier((value,) + earlier)[0]


RING = [(2 * z + y, 2 * ((z + 1) % 4) + y) for z in range(4) for y in range(2)]


def in_order(blocks, z, rows):
    row = jnp.concatenate([blocks[3], blocks[2], blocks[1], blocks[0], blocks[3], blocks[2], blocks[1]])
    return lax.dynamic_slice_in_dim(row, (3 - z) * rows, 4 * rows, axis=0)


ORDER = (
    ("q", "z"), ("k", "y"), ("o", "z"), ("u", "y"), ("d", "z"), ("k", "z"), ("q", "z"), ("o", "z"),
    ("k", "z"), ("q", "z"), ("d", "z"), ("o", "z"), ("k", "z"), ("q", "y"), ("d", "z"), ("o", "y"),
    ("g", "z"), ("u", "z"), ("d", "y"), ("g", "z"), ("u", "z"), ("g", "z"), ("u", "z"), ("g", "y"),
)
WINDOW = 6


def gather_rep(blocks):
    if lax.axis_size("rep") != 8:
        return {n: lax.all_gather(x, "rep", axis=0, tiled=True) for n, x in blocks.items()}, {}
    place = lax.axis_index("rep")
    z, even = place // 2, place % 2 == 0
    chain = {name: [block] for name, block in blocks.items()}
    result, steps, named = {}, [], {}
    for index, (name, kind) in enumerate(ORDER):
        held = chain[name]
        rows, columns = blocks[name].shape
        if kind == "z":
            value, pairs = held[-1], RING
        else:
            value = in_order(held, z, rows) if len(held) == 4 else held[0]
            pairs = xor_perm(8, 1)
        if index >= WINDOW:
            value = after(value, *steps[max(0, index - WINDOW - 2) : index - WINDOW + 1])
        got = lax.ppermute(value, "rep", pairs)
        steps.append(got)
        named[name, kind, len(held)] = got
        if kind == "z":
            held.append(got)
            if len(held) == 4 and held[0].shape[0] == 2 * rows:
                result[name] = in_order(held, z, 2 * rows)
        elif len(held) == 4:
            value, got = value.reshape(4, rows, columns), got.reshape(4, rows, columns)
            both = [jnp.where(even, value, got), jnp.where(even, got, value)]
            result[name] = jnp.stack(both, axis=1).reshape(8 * rows, columns)
        else:
            chain[name] = [
                jnp.where(even, jnp.concatenate([value, got]), jnp.concatenate([got, value]))
            ]
    return result, named


def as_bf(value):
    return value.astype(jnp.bfloat16)


class RepSum:
    def __init__(self, partial, ring_first):
        self.count = 0
        self.whole = lax.axis_size("rep") != 8
        if self.whole:
            self.total = lax.psum_scatter(partial, "rep", scatter_dimension=0, tiled=True)
            return
        rows, columns = partial.shape[0] // 8, partial.shape[1]
        place = lax.axis_index("rep")
        self.z, self.y = place // 2, place % 2
        self.kinds = "zzzy" if ring_first else "yzzz"
        self.held = partial.reshape(4, 2, rows, columns)
        self.axis, self.got = 1, None

    def entry(self, back):
        return lax.dynamic_index_in_dim(self.held, (self.z + 4 - back) % 4, axis=0, keepdims=False)

    def step(self, *ahead):
        if self.whole:
            return self.total
        kind = self.kinds[self.count]
        if kind == "z":
            back = self.kinds[: self.count].count("z") + 1
            value = self.entry(back)
            if back > 1:
                value = value + self.got.astype(jnp.float32)
            self.got = lax.ppermute(after(as_bf(value), *ahead), "rep", RING)
            came = self.got
            if back == 3:
                self.held = self.entry(0) + self.got.astype(jnp.float32)
                self.axis = 0
        else:
            value = lax.dynamic_index_in_dim(self.held, 1 - self.y, axis=self.axis, keepdims=False)
            came = lax.ppermute(after(as_bf(value), *ahead), "rep", xor_perm(8, 1))
            kept = lax.dynamic_index_in_dim(self.held, self.y, axis=self.axis, keepdims=False)
            self.held = kept + came.astype(jnp.float32)
        self.count += 1
        self.total = self.held
        return came


def columns_of(array, widths, index):
    start, parts = 0, []
    for width in widths:
        parts.append(
            lax.dynamic_slice_in_dim(array, start + index * (width // 4), width // 4, axis=1)
        )
        start += width
    return jnp.concatenate(parts, axis=1)


def trade(pieces):
    return [pieces(0)] + [lax.ppermute(pieces(k), "shard", xor_perm(4, k)) for k in (1, 2, 3)]


def arrange(parts, mine):
    odd, high = mine % 2 == 1, mine // 2 == 1
    a, b, c, d = parts
    a, b, c, d = (
        jnp.where(odd, b, a),
        jnp.where(odd, a, b),
        jnp.where(odd, d, c),
        jnp.where(odd, c, d),
    )
    return [jnp.where(high, c, a), jnp.where(high, d, b), jnp.where(high, a, c), jnp.where(high, b, d)]


def split_columns(array, widths, extra=None, ahead=()):
    mine = lax.axis_index("shard")

    def pieces(k):
        piece = columns_of(array, widths, mine ^ k)
        if extra is not None:
            piece = jnp.concatenate([piece, extra], axis=1)
        return after(piece, *ahead) if k else piece

    parts = trade(pieces)
    return jnp.concatenate(arrange(parts, mine)), parts[3]


def join_columns(array, widths, gains=None):
    rows = array.shape[0] // 4
    mine = lax.axis_index("shard")

    def pieces(k):
        piece = lax.dynamic_slice_in_dim(array, (mine ^ k) * rows, rows, axis=0)
        if gains is not None:
            row = lax.dynamic_slice_in_dim(gains, mine ^ k, 1, axis=0)
            row = jnp.pad(row, ((0, 15), (0, piece.shape[1] - row.shape[1])))
            piece = jnp.concatenate([piece, row])
        return as_bf(piece) if k else piece

    parts = [piece.astype(jnp.float32) for piece in trade(pieces)]
    columns, start = [], 0
    ordered = arrange([part[:rows] for part in parts], mine)
    for width in widths:
        columns += [part[:, start : start + width // 4] for part in ordered]
        start += width // 4
    joined = jnp.concatenate(columns, axis=1)
    if gains is None:
        return joined
    return joined, sum(part[rows, : gains.shape[1]] for part in parts)


def turned(inverse):
    rep, shard = lax.axis_size("rep"), lax.axis_size("shard")
    pairs = [(b, (b % rep) * shard + b // rep) for b in range(rep * shard)]
    return [(b, a) for a, b in pairs] if inverse else pairs


QKV_WIDTHS = (QUERY_HEADS * HEAD_SIZE, KEY_VALUE_HEADS * HEAD_SIZE, KEY_VALUE_HEADS * HEAD_SIZE)
GATE_UP_WIDTHS = (FF, FF)


def dot(left, right):
    return jnp.dot(left, right, preferred_element_type=jnp.float32)


def dot_t(left, right):
    return lax.dot_general(left, right, (((1,), (1,)), ((), ())), preferred_element_type=jnp.float32)


def t_dot(left, right):
    return lax.dot_general(left, right, (((0,), (0,)), ((), ())), preferred_element_type=jnp.float32)


def inverse_rms(signal):
    return lax.rsqrt(jnp.mean(signal * signal, axis=-1, keepdims=True) + NORM_EPS)


def turn_tables(length):
    half = HEAD_SIZE // 2
    freqs = np.exp(-math.log(ROPE_BASE) * 2.0 * np.arange(half) / HEAD_SIZE).astype(np.float32)
    angles = (np.arange(length, dtype=np.float32)[:, None] * freqs[None, :]).astype(np.float64)
    cosine, sine = np.cos(angles), np.sin(angles)
    return (
        jnp.asarray(np.concatenate([cosine, cosine], 1), jnp.float32),
        jnp.asarray(np.concatenate([-sine, sine], 1), jnp.float32),
    )


def swap_halves(signal):
    return pltpu.roll(signal, HEAD_SIZE // 2, 1)


def allowed_pairs(segment_row):
    length = segment_row.shape[1]
    across = jnp.broadcast_to(segment_row, (length, length))
    rows = lax.broadcasted_iota(jnp.int32, (length, length), 0)
    columns = lax.broadcasted_iota(jnp.int32, (length, length), 1)
    return (columns <= rows) & (across == across.T)


KV_LOCAL = KEY_VALUE_HEADS // 4
GROUP = QUERY_HEADS // KEY_VALUE_HEADS
SCALE = 1.0 / math.sqrt(HEAD_SIZE)


def head_columns(head):
    return slice(head * HEAD_SIZE, (head + 1) * HEAD_SIZE)


def rotate_key(kv_ref, rows, head, gain, cosine, sine):
    keys = kv_ref[rows, head_columns(head)]
    inverse = inverse_rms(keys)
    normed = keys * inverse * gain
    k_rot = as_bf(normed * cosine + swap_halves(normed) * sine)
    return keys, inverse, k_rot, as_bf(kv_ref[rows, head_columns(KV_LOCAL + head)])


def rotate_query(q_ref, rows, head, gain, cosine, sine):
    queries = q_ref[rows, head_columns(head)]
    inverse = inverse_rms(queries)
    normed = queries * inverse * gain
    return queries, inverse, as_bf((normed * cosine + swap_halves(normed) * sine) * SCALE)


def probabilities(q_rot, k_rot, allowed):
    scores = jnp.where(allowed, dot_t(q_rot, k_rot), -1e30)
    peak = jnp.max(scores, axis=-1, keepdims=True)
    log_total = peak + jnp.log(jnp.sum(jnp.exp(scores - peak), axis=-1, keepdims=True))
    return jnp.exp(scores - log_total)


def block_rows(index, length):
    return pl.ds(pl.multiple_of(index * length, length), length)


def emit_partial(partial, send_ref, keep_ref):
    length = send_ref.shape[1]
    keep_ref[0] = partial[:length]
    keep_ref[1] = partial[2 * length : 3 * length]
    send_ref[0] = as_bf(partial[3 * length :])
    send_ref[1] = as_bf(partial[length : 2 * length])


def attention_kernel(
    tok0, tok1, tok2, tok3, seg_ref, gain_ref, cos_ref, sin_ref, wq_ref, wk_ref, wo_ref,
    normed_ref, q_ref, kv_ref, att_ref, send_ref, keep_ref,
):
    length = send_ref.shape[1]
    attn_gain = gain_ref[:, :D]
    query_gain = gain_ref[:, 2 * D : 2 * D + HEAD_SIZE]
    key_gain = gain_ref[:, 2 * D + HEAD_SIZE :]
    for k, ref in enumerate((tok0, tok1, tok2, tok3)):
        tokens = ref[:length].astype(jnp.float32)
        normed_ref[k * length : (k + 1) * length] = as_bf(tokens * inverse_rms(tokens) * attn_gain)
    q_ref[...] = dot(normed_ref[...], wq_ref[...])
    kv_ref[...] = dot(normed_ref[...], wk_ref[:, : kv_ref.shape[1]])

    def one_row(row, carry):
        rows = block_rows(row, length)
        cosine, sine = cos_ref[...], sin_ref[...]
        allowed = allowed_pairs(seg_ref[pl.ds(row, 1), :])
        for c in range(KV_LOCAL):
            _, _, k_rot, v_bf = rotate_key(kv_ref, rows, c, key_gain, cosine, sine)
            for head in range(c * GROUP, (c + 1) * GROUP):
                _, _, q_rot = rotate_query(q_ref, rows, head, query_gain, cosine, sine)
                probs = as_bf(probabilities(q_rot, k_rot, allowed))
                att_ref[rows, head_columns(head)] = as_bf(dot(probs, v_bf))
        return carry

    lax.fori_loop(0, 4, one_row, 0)
    emit_partial(dot(att_ref[...], wo_ref[...]), send_ref, keep_ref)


def attention_back_kernel(
    dmid_ref, tok0, tok1, tok2, tok3, seg_ref, gain_ref, cos_ref, sin_ref, q_ref, kv_ref, wq_ref, wk_ref,
    wo_ref, dq_ref, dkv_ref, dgain_ref, dattn_ref, send_ref, keep_ref, datt_ref,
):
    length = send_ref.shape[1]
    query_gain = gain_ref[:, 2 * D : 2 * D + HEAD_SIZE]
    key_gain = gain_ref[:, 2 * D + HEAD_SIZE :]
    datt_ref[...] = as_bf(dot_t(dmid_ref[...], wo_ref[...]))

    def one_row(row, carry):
        d_query_gain, d_key_gain = carry
        rows = block_rows(row, length)
        cosine, sine = cos_ref[...], sin_ref[...]
        allowed = allowed_pairs(seg_ref[pl.ds(row, 1), :])
        for c in range(KV_LOCAL):
            keys, inv_key, k_rot, v_bf = rotate_key(kv_ref, rows, c, key_gain, cosine, sine)
            d_values = jnp.zeros((length, HEAD_SIZE), jnp.float32)
            d_krot = jnp.zeros((length, HEAD_SIZE), jnp.float32)
            for head in range(c * GROUP, (c + 1) * GROUP):
                queries, inv_query, q_rot = rotate_query(q_ref, rows, head, query_gain, cosine, sine)
                probs = probabilities(q_rot, k_rot, allowed)
                probs_bf = as_bf(probs)
                d_att = datt_ref[rows, head_columns(head)]
                attended = dot(probs_bf, v_bf)
                delta = jnp.sum(d_att.astype(jnp.float32) * attended, axis=-1, keepdims=True)
                d_scores = as_bf(probs * (dot_t(d_att, v_bf) - delta))
                d_values = d_values + t_dot(probs_bf, d_att)
                d_krot = d_krot + t_dot(d_scores, q_rot)
                upstream = dot(d_scores, k_rot) * SCALE
                upstream = upstream * cosine - swap_halves(upstream) * sine
                d_queries, d_gain = rms_backward(queries, inv_query, query_gain, upstream)
                dq_ref[rows, head_columns(head)] = as_bf(d_queries)
                d_query_gain = d_query_gain + d_gain[None]
            upstream = d_krot * cosine - swap_halves(d_krot) * sine
            d_keys, d_gain = rms_backward(keys, inv_key, key_gain, upstream)
            dkv_ref[rows, head_columns(c)] = as_bf(d_keys)
            dkv_ref[rows, head_columns(KV_LOCAL + c)] = as_bf(d_values)
            d_key_gain = d_key_gain + d_gain[None]
        return d_query_gain, d_key_gain

    zero = jnp.zeros((1, HEAD_SIZE), jnp.float32)
    d_query_gain, d_key_gain = lax.fori_loop(0, 4, one_row, (zero, zero))
    dgain_ref[0:1] = d_query_gain
    dgain_ref[1:2] = d_key_gain
    partial = dot_t(dq_ref[...], wq_ref[...]) + dot_t(dkv_ref[...], wk_ref[:, : kv_ref.shape[1]])
    emit_partial(partial, send_ref, keep_ref)
    d_attn_gain = jnp.zeros((1, D), jnp.float32)
    for k, ref in enumerate((tok0, tok1, tok2, tok3)):
        tokens = ref[:length].astype(jnp.float32)
        scaled = tokens * inverse_rms(tokens)
        part = partial[k * length : (k + 1) * length] * scaled
        d_attn_gain = d_attn_gain + jnp.sum(part, axis=0, keepdims=True)
    dattn_ref[...] = d_attn_gain


def ffn_kernel(
    mn0, mn1, mn2, mn3, cot0, cot1, cot2, cot3, gate_ref, up_ref, down_ref,
    mn_ref, cot_ref, hid_ref, dgate_ref, dup_ref, send_ref, keep_ref,
):
    length = send_ref.shape[1]
    for k, (mn, cot) in enumerate(zip((mn0, mn1, mn2, mn3), (cot0, cot1, cot2, cot3))):
        mn_ref[k * length : (k + 1) * length] = mn[...]
        cot_ref[k * length : (k + 1) * length] = cot[...]

    def half(index, carry):
        rows = block_rows(index, 2 * length)
        gate_pre = dot(mn_ref[rows], gate_ref[...])
        up_pre = dot(mn_ref[rows], up_ref[...])
        d_hidden = dot_t(cot_ref[rows], down_ref[...])
        sig = jax.nn.sigmoid(gate_pre)
        hid_ref[rows] = as_bf(gate_pre * sig * up_pre)
        dgate_ref[rows] = as_bf(d_hidden * up_pre * sig * (1.0 + gate_pre * (1.0 - sig)))
        dup_ref[rows] = as_bf(d_hidden * gate_pre * sig)
        return carry

    lax.fori_loop(0, 2, half, 0)
    emit_partial(
        dot_t(dgate_ref[...], gate_ref[...]) + dot_t(dup_ref[...], up_ref[...]), send_ref, keep_ref
    )


def run_kernel(kernel, outputs, *inputs, scratch=()):
    whole = pl.BlockSpec(memory_space=pltpu.VMEM)
    return pl.pallas_call(
        kernel,
        out_shape=[jax.ShapeDtypeStruct(shape, dtype) for shape, dtype in outputs],
        in_specs=[whole] * len(inputs),
        out_specs=[whole] * len(outputs),
        scratch_shapes=scratch,
        compiler_params=pltpu.CompilerParams(vmem_limit_bytes=48 * 1024 * 1024),
    )(*inputs)


def adamw(weight, grad_sum, mean_old, square_old, step_float, token_total, decay):
    gradient = grad_sum / token_total
    mean_new = BETA_ONE * mean_old + (1.0 - BETA_ONE) * gradient
    square_new = BETA_TWO * square_old + (1.0 - BETA_TWO) * gradient * gradient
    fix_one = 1.0 - jnp.power(BETA_ONE, step_float)
    fix_two = 1.0 - jnp.power(BETA_TWO, step_float)
    change = mean_new / fix_one / (jnp.sqrt(square_new / fix_two) + ADAM_EPS) + decay * weight
    return (weight - LEARN_RATE * change, mean_new, square_new)


def body(
    tokens,
    segments,
    out_cot,
    step_count,
    w_qkv,
    w_out,
    w_gate_up,
    w_down,
    norm_gains,
    mean_qkv,
    mean_out,
    mean_gate_up,
    mean_down,
    mean_gains,
    square_qkv,
    square_out,
    square_gate_up,
    square_down,
    square_gains,
):
    length = tokens.shape[0]
    bf = jnp.bfloat16
    both = ("rep", "shard")
    mine = lax.axis_index("shard")
    own = norm_gains.shape[0]
    extra = jnp.pad(norm_gains.astype(bf)[None], ((0, w_qkv.shape[0] - 1), (0, 128 - own)))
    split, first = split_columns(w_qkv.astype(bf), QKV_WIDTHS, extra)
    turned_out = lax.ppermute(w_out.astype(bf), both, turned(False))
    split_ff, _ = split_columns(w_gate_up.astype(bf), GATE_UP_WIDTHS, ahead=(first,))
    turned_down = lax.ppermute(after(w_down.astype(bf), first), both, turned(False))
    wide, half = QUERY_HEADS * HEAD_SIZE // 4, FF // 4
    whole, steps = gather_rep(
        {
            "q": split[:, :wide],
            "k": split[:, wide:],
            "o": turned_out,
            "g": split_ff[:, :half],
            "u": split_ff[:, half:],
            "d": turned_down,
        }
    )
    w_query, output, gate, up, down = (whole[n] for n in "qogud")
    w_keys = whole["k"]
    gains = w_keys.reshape(-1, w_qkv.shape[0], w_keys.shape[1])
    gains = gains[:, 0, w_keys.shape[1] - 128 : w_keys.shape[1] - 128 + own]
    gains = gains.reshape(1, -1).astype(jnp.float32)
    marks = lax.dynamic_update_slice(jnp.zeros((16, D), bf), segments.astype(bf), (0, 0))
    group = jnp.concatenate([tokens, marks])
    def seen(*events):
        return tuple(steps[event] for event in events if event in steps)

    group = group_gather(after(group, *seen(("q", "z", 1))))
    segment_group = jnp.concatenate([part[length : length + 1, :length] for part in group])
    segment_group = segment_group.astype(jnp.float32)
    attn_gain, mlp_gain = gains[0, :D], gains[0, D : 2 * D]
    cosine, sine = turn_tables(length)
    flat, kv_width = 4 * length, w_keys.shape[1] - 128
    sent = [((2, length, D), bf), ((2, length, D), jnp.float32)]

    x_float = tokens.astype(jnp.float32)
    inv_attn = rms_forward(x_float, attn_gain)[1]
    normed, queries, keys_values, attended_bf, *partial = run_kernel(
        attention_kernel,
        [((flat, D), bf), ((flat, wide), jnp.float32), ((flat, kv_width), jnp.float32), ((flat, wide), bf)]
        + sent,
        *group, segment_group, gains, cosine, sine, w_query, w_keys, output,
    )
    send = after(partial[0], *seen(("g", "z", 2), ("u", "z", 1)))
    cot_group = group_gather(after(out_cot, send))
    x_mid = x_float + group_sum(send, partial[1])
    mid_float, inv_mlp = rms_forward(x_mid, mlp_gain)
    mid_normed, cot_all, hidden, d_gate, d_up, *partial = run_kernel(
        ffn_kernel,
        [((flat, D), bf), ((flat, D), bf)] + [((flat, half), bf)] * 3 + sent,
        *group_gather(after(mid_float.astype(bf), *seen(("g", "z", 3), ("u", "z", 2)))),
        *cot_group, gate, up, down,
    )
    rep_down = RepSum(dot(hidden.T, cot_all), True)
    rep_up = RepSum(dot(mid_normed.T, d_up), True)
    rep_gate = RepSum(dot(mid_normed.T, d_gate), False)
    first = rep_down.step(), rep_gate.step(), rep_up.step()
    d_mid_norm = group_sum(*partial)
    d_mid_part, d_mlp_gain = rms_backward(x_mid, inv_mlp, mlp_gain, d_mid_norm)
    d_mid = out_cot.astype(jnp.float32) + d_mid_part
    second = rep_down.step(), rep_up.step()
    d_mid_bf = jnp.concatenate(group_gather(d_mid.astype(bf)))
    rep_out = RepSum(dot(attended_bf.T, d_mid_bf), False)
    rep_down.step(d_mid_bf), rep_up.step(d_mid_bf), rep_gate.step(d_mid_bf), rep_out.step()
    d_query, d_keys, d_head_gains, d_attn_gain, *partial = run_kernel(
        attention_back_kernel,
        [((flat, wide), bf), ((flat, kv_width), bf), ((2, HEAD_SIZE), jnp.float32), ((1, D), jnp.float32)]
        + sent,
        after(d_mid_bf, first[1], *second),
        *group, segment_group, gains, cosine, sine, queries, keys_values, w_query, w_keys, output,
        scratch=[pltpu.VMEM((flat, wide), bf)],
    )

    gain_grads = jnp.concatenate([d_attn_gain[0], d_mlp_gain, d_head_gains.reshape(-1)])
    gain_grads = gain_grads.reshape(-1, 1, 4 * own)
    gain_grads = jnp.pad(gain_grads, ((0, 0), (0, 15), (0, kv_width - 4 * own)))
    grad_keys = dot(normed.T, d_keys).reshape(gain_grads.shape[0], -1, kv_width)
    rep_keys = RepSum(jnp.concatenate([grad_keys, gain_grads], axis=1).reshape(-1, kv_width), True)
    rep_query = RepSum(dot(normed.T, d_query), False)
    begun = rep_keys.step(), rep_query.step()
    for _ in range(3):
        rep_keys.step(), rep_query.step()
    for ready in (rep_gate, rep_gate, rep_out, rep_up, rep_down, rep_out, rep_out):
        ready.step(begun[0])
    sum_keys, sum_query = rep_keys.total, rep_query.total
    group_rows = grad_keys.shape[1]
    sum_qkv, sum_gain = join_columns(
        jnp.concatenate([sum_query, sum_keys[:group_rows]], axis=1),
        QKV_WIDTHS,
        sum_keys[group_rows, : 4 * own].reshape(4, own),
    )
    d_normed = group_sum(*partial)
    input_grad = d_mid + rms_backward(x_float, inv_attn, attn_gain, d_normed)[0]
    partial = dot(hidden, down).reshape(4, length, D)
    send = after(as_bf(jnp.stack([partial[3], partial[1]])), begun[0])
    layer_out = (x_mid + group_sum(send, (partial[0], partial[2]))).astype(bf)
    sum_gate_up = join_columns(jnp.concatenate([rep_gate.total, rep_up.total], axis=1), GATE_UP_WIDTHS)
    sum_down = lax.ppermute(as_bf(rep_down.total), both, turned(True)).astype(jnp.float32)
    sum_out = lax.ppermute(as_bf(rep_out.total), both, turned(True)).astype(jnp.float32)

    token_total = float(length * lax.axis_size(both))
    step_float = step_count[0].astype(jnp.float32)
    new_qkv, new_mean_qkv, new_square_qkv = adamw(
        w_qkv, sum_qkv, mean_qkv, square_qkv, step_float, token_total, DECAY_RATE
    )
    new_out, new_mean_out, new_square_out = adamw(
        w_out, sum_out, mean_out, square_out, step_float, token_total, DECAY_RATE
    )
    new_gate_up, new_mean_gate_up, new_square_gate_up = adamw(
        w_gate_up, sum_gate_up, mean_gate_up, square_gate_up, step_float, token_total, DECAY_RATE
    )
    new_down, new_mean_down, new_square_down = adamw(
        w_down, sum_down, mean_down, square_down, step_float, token_total, DECAY_RATE
    )
    new_gains, new_mean_gains, new_square_gains = adamw(
        norm_gains, sum_gain, mean_gains, square_gains, step_float, token_total, 0.0
    )
    return (
        layer_out,
        input_grad,
        sum_qkv,
        sum_out,
        sum_gate_up,
        sum_down,
        sum_gain,
        new_qkv,
        new_out,
        new_gate_up,
        new_down,
        new_gains,
        new_mean_qkv,
        new_mean_out,
        new_mean_gate_up,
        new_mean_down,
        new_mean_gains,
        new_square_qkv,
        new_square_out,
        new_square_gate_up,
        new_square_down,
        new_square_gains,
    )


def solution(mesh):
    return jax.shard_map(
        body,
        mesh=mesh,
        in_specs=(
            P(("rep", "shard"), None),
            P(("rep", "shard"), None),
            P(("rep", "shard"), None),
            P(),
            P(("rep", "shard"), None),
            P(("rep", "shard"), None),
            P(("rep", "shard"), None),
            P(("rep", "shard"), None),
            P(("rep", "shard")),
            P(("rep", "shard"), None),
            P(("rep", "shard"), None),
            P(("rep", "shard"), None),
            P(("rep", "shard"), None),
            P(("rep", "shard")),
            P(("rep", "shard"), None),
            P(("rep", "shard"), None),
            P(("rep", "shard"), None),
            P(("rep", "shard"), None),
            P(("rep", "shard")),
        ),
        out_specs=(
            P(("rep", "shard"), None),
            P(("rep", "shard"), None),
            P(("rep", "shard"), None),
            P(("rep", "shard"), None),
            P(("rep", "shard"), None),
            P(("rep", "shard"), None),
            P(("rep", "shard")),
            P(("rep", "shard"), None),
            P(("rep", "shard"), None),
            P(("rep", "shard"), None),
            P(("rep", "shard"), None),
            P(("rep", "shard")),
            P(("rep", "shard"), None),
            P(("rep", "shard"), None),
            P(("rep", "shard"), None),
            P(("rep", "shard"), None),
            P(("rep", "shard")),
            P(("rep", "shard"), None),
            P(("rep", "shard"), None),
            P(("rep", "shard"), None),
            P(("rep", "shard"), None),
            P(("rep", "shard")),
        ),
        check_vma=False,
    )
```

```python
import functools
import math

import jax
import jax.numpy as jnp
import numpy as np
from jax import lax
from jax.experimental import pallas as pl
from jax.experimental.pallas import tpu as pltpu
from jax.sharding import PartitionSpec as P

D = 1024
QUERY_HEADS = 16
KEY_VALUE_HEADS = 8
HEAD_SIZE = 128
FF = 3072


NORM_EPS = 1e-06
ROPE_BASE = 1000000.0
LEARN_RATE = 0.02
BETA_ONE = 0.9
BETA_TWO = 0.95
ADAM_EPS = 1e-08
DECAY_RATE = 0.1


def rms_forward(signal, gain):
    inverse = lax.rsqrt(jnp.mean(signal * signal, axis=-1, keepdims=True) + NORM_EPS)
    return (signal * inverse * gain, inverse)


def rms_backward(signal, inverse, gain, upstream):
    scaled = upstream * gain
    inner = jnp.mean(scaled * signal, axis=-1, keepdims=True)
    d_signal = inverse * (scaled - signal * inverse * inverse * inner)
    d_gain = jnp.sum((upstream * signal * inverse).reshape(-1, signal.shape[-1]), axis=0)
    return (d_signal, d_gain)


def xor_perm(axis_size, bit):
    return [(i, i ^ bit) for i in range(axis_size)]


def group_gather(part):
    near = lax.ppermute(part, "shard", xor_perm(4, 1))
    far = lax.ppermute(part, "shard", xor_perm(4, 2))
    return part, near, far, lax.ppermute(far, "shard", xor_perm(4, 1))


def group_sum(send, keep):
    near = lax.ppermute(send, "shard", xor_perm(4, 1))
    far = lax.ppermute(as_bf(keep[1] + near[0].astype(jnp.float32)), "shard", xor_perm(4, 2))
    return keep[0] + near[1].astype(jnp.float32) + far.astype(jnp.float32)


def after(value, *earlier):
    if not earlier:
        return value
    return lax.optimization_barrier((value,) + earlier)[0]


RING = [(2 * z + y, 2 * ((z + 1) % 4) + y) for z in range(4) for y in range(2)]


def in_order(blocks, z, rows):
    row = jnp.concatenate([blocks[3], blocks[2], blocks[1], blocks[0], blocks[3], blocks[2], blocks[1]])
    return lax.dynamic_slice_in_dim(row, (3 - z) * rows, 4 * rows, axis=0)


ORDER = (
    ("q", "z"), ("k", "y"), ("o", "z"), ("u", "y"), ("d", "z"), ("k", "z"), ("q", "z"), ("o", "z"),
    ("k", "z"), ("q", "z"), ("d", "z"), ("o", "z"), ("k", "z"), ("q", "y"), ("d", "z"), ("o", "y"),
    ("g", "z"), ("u", "z"), ("d", "y"), ("g", "z"), ("u", "z"), ("g", "z"), ("u", "z"), ("g", "y"),
)
WINDOW = 6


def finish_ring(held, z, rows, *ahead):
    return in_order(held[:-1] + [after(held[-1], *ahead)], z, rows)


def finish_pair(value, got, even, rows, *ahead):
    got = after(got, *ahead)
    columns = value.shape[1]
    value, got = value.reshape(4, rows, columns), got.reshape(4, rows, columns)
    both = [jnp.where(even, value, got), jnp.where(even, got, value)]
    return jnp.stack(both, axis=1).reshape(8 * rows, columns)


def gathered(whole, *ahead):
    return lax.all_gather(whole, "rep", axis=0, tiled=True)


def gather_rep(blocks):
    if lax.axis_size("rep") != 8:
        return {n: functools.partial(gathered, x) for n, x in blocks.items()}, {}
    place = lax.axis_index("rep")
    z, even = place // 2, place % 2 == 0
    chain = {name: [block] for name, block in blocks.items()}
    result, steps, named = {}, [], {}
    for index, (name, kind) in enumerate(ORDER):
        held = chain[name]
        rows, columns = blocks[name].shape
        if kind == "z":
            value, pairs = held[-1], RING
        else:
            value = in_order(held, z, rows) if len(held) == 4 else held[0]
            pairs = xor_perm(8, 1)
        if index >= WINDOW:
            value = after(value, *steps[max(0, index - WINDOW - 3) : index - WINDOW + 1])
        got = lax.ppermute(value, "rep", pairs)
        steps.append(got)
        named[name, kind, len(held)] = got
        if kind == "z":
            held.append(got)
            if len(held) == 4 and held[0].shape[0] == 2 * rows:
                result[name] = functools.partial(finish_ring, held, z, 2 * rows)
        elif len(held) == 4:
            result[name] = functools.partial(finish_pair, value, got, even, rows)
        else:
            chain[name] = [
                jnp.where(even, jnp.concatenate([value, got]), jnp.concatenate([got, value]))
            ]
    return result, named


def as_bf(value):
    return value.astype(jnp.bfloat16)


class RepSum:
    def __init__(self, partial, ring_first):
        self.count = 0
        self.whole = lax.axis_size("rep") != 8
        if self.whole:
            self.total = lax.psum_scatter(partial, "rep", scatter_dimension=0, tiled=True)
            return
        rows, columns = partial.shape[0] // 8, partial.shape[1]
        place = lax.axis_index("rep")
        self.z, self.y = place // 2, place % 2
        self.kinds = "zzzy" if ring_first else "yzzz"
        self.held = partial.reshape(4, 2, rows, columns)
        self.axis, self.got = 1, None

    def entry(self, back):
        return lax.dynamic_index_in_dim(self.held, (self.z + 4 - back) % 4, axis=0, keepdims=False)

    def pending(self):
        if self.whole:
            return self.total
        if self.kinds[self.count] == "y":
            return as_bf(lax.dynamic_index_in_dim(self.held, 1 - self.y, axis=self.axis, keepdims=False))
        back = self.kinds[: self.count].count("z") + 1
        value = self.entry(back)
        return as_bf(value if back == 1 else value + self.got.astype(jnp.float32))

    def step(self, *ahead):
        if self.whole:
            return self.total
        kind, value = self.kinds[self.count], self.pending()
        if kind == "z":
            back = self.kinds[: self.count].count("z") + 1
            self.got = lax.ppermute(after(value, *ahead), "rep", RING)
            came = self.got
            if back == 3:
                self.held = self.entry(0) + self.got.astype(jnp.float32)
                self.axis = 0
        else:
            came = lax.ppermute(after(value, *ahead), "rep", xor_perm(8, 1))
            kept = lax.dynamic_index_in_dim(self.held, self.y, axis=self.axis, keepdims=False)
            self.held = kept + came.astype(jnp.float32)
        self.count += 1
        self.total = self.held
        return came


def columns_of(array, widths, index):
    start, parts = 0, []
    for width in widths:
        parts.append(
            lax.dynamic_slice_in_dim(array, start + index * (width // 4), width // 4, axis=1)
        )
        start += width
    return jnp.concatenate(parts, axis=1)


def trade(pieces):
    return [pieces(0)] + [lax.ppermute(pieces(k), "shard", xor_perm(4, k)) for k in (1, 2, 3)]


def arrange(parts, mine):
    odd, high = mine % 2 == 1, mine // 2 == 1
    a, b, c, d = parts
    a, b, c, d = (
        jnp.where(odd, b, a),
        jnp.where(odd, a, b),
        jnp.where(odd, d, c),
        jnp.where(odd, c, d),
    )
    return [jnp.where(high, c, a), jnp.where(high, d, b), jnp.where(high, a, c), jnp.where(high, b, d)]


def split_columns(array, widths, extra=None, ahead=()):
    mine = lax.axis_index("shard")

    def pieces(k):
        piece = columns_of(array, widths, mine ^ k)
        if extra is not None:
            piece = jnp.concatenate([piece, extra], axis=1)
        return after(piece, *ahead) if k else piece

    parts = trade(pieces)
    return jnp.concatenate(arrange(parts, mine)), parts[3]


def join_columns(array, widths, gains=None):
    rows = array.shape[0] // 4
    mine = lax.axis_index("shard")

    def pieces(k):
        piece = lax.dynamic_slice_in_dim(array, (mine ^ k) * rows, rows, axis=0)
        if gains is not None:
            row = lax.dynamic_slice_in_dim(gains, mine ^ k, 1, axis=0)
            row = jnp.pad(row, ((0, 15), (0, piece.shape[1] - row.shape[1])))
            piece = jnp.concatenate([piece, row])
        return as_bf(piece) if k else piece

    parts = [piece.astype(jnp.float32) for piece in trade(pieces)]
    columns, start = [], 0
    ordered = arrange([part[:rows] for part in parts], mine)
    for width in widths:
        columns += [part[:, start : start + width // 4] for part in ordered]
        start += width // 4
    joined = jnp.concatenate(columns, axis=1)
    if gains is None:
        return joined
    return joined, sum(part[rows, : gains.shape[1]] for part in parts)


def turned(inverse):
    rep, shard = lax.axis_size("rep"), lax.axis_size("shard")
    pairs = [(b, (b % rep) * shard + b // rep) for b in range(rep * shard)]
    return [(b, a) for a, b in pairs] if inverse else pairs


QKV_WIDTHS = (QUERY_HEADS * HEAD_SIZE, KEY_VALUE_HEADS * HEAD_SIZE, KEY_VALUE_HEADS * HEAD_SIZE)
GATE_UP_WIDTHS = (FF, FF)


def dot(left, right):
    return jnp.dot(left, right, preferred_element_type=jnp.float32)


def dot_t(left, right):
    return lax.dot_general(left, right, (((1,), (1,)), ((), ())), preferred_element_type=jnp.float32)


def t_dot(left, right):
    return lax.dot_general(left, right, (((0,), (0,)), ((), ())), preferred_element_type=jnp.float32)


def inverse_rms(signal):
    return lax.rsqrt(jnp.mean(signal * signal, axis=-1, keepdims=True) + NORM_EPS)


def turn_tables(length):
    half = HEAD_SIZE // 2
    freqs = np.exp(-math.log(ROPE_BASE) * 2.0 * np.arange(half) / HEAD_SIZE).astype(np.float32)
    angles = (np.arange(length, dtype=np.float32)[:, None] * freqs[None, :]).astype(np.float64)
    cosine, sine = np.cos(angles), np.sin(angles)
    return (
        jnp.asarray(np.concatenate([cosine, cosine], 1), jnp.float32),
        jnp.asarray(np.concatenate([-sine, sine], 1), jnp.float32),
    )


def swap_halves(signal):
    return pltpu.roll(signal, HEAD_SIZE // 2, 1)


def allowed_pairs(segment_row):
    length = segment_row.shape[1]
    across = jnp.broadcast_to(segment_row, (length, length))
    rows = lax.broadcasted_iota(jnp.int32, (length, length), 0)
    columns = lax.broadcasted_iota(jnp.int32, (length, length), 1)
    return (columns <= rows) & (across == across.T)


KV_LOCAL = KEY_VALUE_HEADS // 4
GROUP = QUERY_HEADS // KEY_VALUE_HEADS
SCALE = 1.0 / math.sqrt(HEAD_SIZE)


def head_columns(head):
    return slice(head * HEAD_SIZE, (head + 1) * HEAD_SIZE)


def rotate_key(kv_ref, rows, head, gain, cosine, sine):
    keys = kv_ref[rows, head_columns(head)]
    inverse = inverse_rms(keys)
    normed = keys * inverse * gain
    k_rot = as_bf(normed * cosine + swap_halves(normed) * sine)
    return keys, inverse, k_rot, as_bf(kv_ref[rows, head_columns(KV_LOCAL + head)])


def rotate_query(q_ref, rows, head, gain, cosine, sine):
    queries = q_ref[rows, head_columns(head)]
    inverse = inverse_rms(queries)
    normed = queries * inverse * gain
    return queries, inverse, as_bf((normed * cosine + swap_halves(normed) * sine) * SCALE)


def probabilities(q_rot, k_rot, allowed):
    scores = jnp.where(allowed, dot_t(q_rot, k_rot), -1e30)
    peak = jnp.max(scores, axis=-1, keepdims=True)
    weights = jnp.exp(scores - peak)
    return weights * (1.0 / jnp.sum(weights, axis=-1, keepdims=True))


def block_rows(index, length):
    return pl.ds(pl.multiple_of(index * length, length), length)


def emit_partial(partial, send_ref, keep_ref):
    length = send_ref.shape[1]
    keep_ref[0] = partial[:length]
    keep_ref[1] = partial[2 * length : 3 * length]
    send_ref[0] = as_bf(partial[3 * length :])
    send_ref[1] = as_bf(partial[length : 2 * length])


def attention_kernel(
    tok0, tok1, tok2, tok3, seg_ref, gain_ref, cos_ref, sin_ref, wq_ref, wk_ref, wo_ref,
    normed_ref, q_ref, kv_ref, att_ref, send_ref, keep_ref,
):
    length = send_ref.shape[1]
    attn_gain = gain_ref[:, :D]
    query_gain = gain_ref[:, 2 * D : 2 * D + HEAD_SIZE]
    key_gain = gain_ref[:, 2 * D + HEAD_SIZE :]
    for k, ref in enumerate((tok0, tok1, tok2, tok3)):
        tokens = ref[:length].astype(jnp.float32)
        normed_ref[k * length : (k + 1) * length] = as_bf(tokens * inverse_rms(tokens) * attn_gain)
    q_ref[...] = dot(normed_ref[...], wq_ref[...])
    kv_ref[...] = dot(normed_ref[...], wk_ref[:, : kv_ref.shape[1]])

    def one_row(row, carry):
        rows = block_rows(row, length)
        cosine, sine = cos_ref[...], sin_ref[...]
        allowed = allowed_pairs(seg_ref[pl.ds(row, 1), :])
        for c in range(KV_LOCAL):
            _, _, k_rot, v_bf = rotate_key(kv_ref, rows, c, key_gain, cosine, sine)
            for head in range(c * GROUP, (c + 1) * GROUP):
                _, _, q_rot = rotate_query(q_ref, rows, head, query_gain, cosine, sine)
                probs = as_bf(probabilities(q_rot, k_rot, allowed))
                att_ref[rows, head_columns(head)] = as_bf(dot(probs, v_bf))
        return carry

    lax.fori_loop(0, 4, one_row, 0)
    emit_partial(dot(att_ref[...], wo_ref[...]), send_ref, keep_ref)


def attention_back_kernel(
    dmid_ref, tok0, tok1, tok2, tok3, seg_ref, gain_ref, cos_ref, sin_ref, q_ref, kv_ref, wq_ref, wk_ref,
    wo_ref, dq_ref, dkv_ref, dgain_ref, dattn_ref, send_ref, keep_ref, datt_ref,
):
    length = send_ref.shape[1]
    query_gain = gain_ref[:, 2 * D : 2 * D + HEAD_SIZE]
    key_gain = gain_ref[:, 2 * D + HEAD_SIZE :]
    datt_ref[...] = as_bf(dot_t(dmid_ref[...], wo_ref[...]))

    def one_row(row, carry):
        d_query_gain, d_key_gain = carry
        rows = block_rows(row, length)
        cosine, sine = cos_ref[...], sin_ref[...]
        allowed = allowed_pairs(seg_ref[pl.ds(row, 1), :])
        for c in range(KV_LOCAL):
            keys, inv_key, k_rot, v_bf = rotate_key(kv_ref, rows, c, key_gain, cosine, sine)
            d_values = jnp.zeros((length, HEAD_SIZE), jnp.float32)
            d_krot = jnp.zeros((length, HEAD_SIZE), jnp.float32)
            for head in range(c * GROUP, (c + 1) * GROUP):
                queries, inv_query, q_rot = rotate_query(q_ref, rows, head, query_gain, cosine, sine)
                probs = probabilities(q_rot, k_rot, allowed)
                probs_bf = as_bf(probs)
                d_att = datt_ref[rows, head_columns(head)]
                d_probs = dot_t(d_att, v_bf)
                delta = jnp.sum(probs_bf.astype(jnp.float32) * d_probs, axis=-1, keepdims=True)
                d_scores = as_bf(probs * (d_probs - delta))
                d_values = d_values + t_dot(probs_bf, d_att)
                d_krot = d_krot + t_dot(d_scores, q_rot)
                upstream = dot(d_scores, k_rot) * SCALE
                upstream = upstream * cosine - swap_halves(upstream) * sine
                d_queries, d_gain = rms_backward(queries, inv_query, query_gain, upstream)
                dq_ref[rows, head_columns(head)] = as_bf(d_queries)
                d_query_gain = d_query_gain + d_gain[None]
            upstream = d_krot * cosine - swap_halves(d_krot) * sine
            d_keys, d_gain = rms_backward(keys, inv_key, key_gain, upstream)
            dkv_ref[rows, head_columns(c)] = as_bf(d_keys)
            dkv_ref[rows, head_columns(KV_LOCAL + c)] = as_bf(d_values)
            d_key_gain = d_key_gain + d_gain[None]
        return d_query_gain, d_key_gain

    zero = jnp.zeros((1, HEAD_SIZE), jnp.float32)
    d_query_gain, d_key_gain = lax.fori_loop(0, 4, one_row, (zero, zero))
    dgain_ref[0:1] = d_query_gain
    dgain_ref[1:2] = d_key_gain
    partial = dot_t(dq_ref[...], wq_ref[...]) + dot_t(dkv_ref[...], wk_ref[:, : kv_ref.shape[1]])
    emit_partial(partial, send_ref, keep_ref)
    d_attn_gain = jnp.zeros((1, D), jnp.float32)
    for k, ref in enumerate((tok0, tok1, tok2, tok3)):
        tokens = ref[:length].astype(jnp.float32)
        scaled = tokens * inverse_rms(tokens)
        part = partial[k * length : (k + 1) * length] * scaled
        d_attn_gain = d_attn_gain + jnp.sum(part, axis=0, keepdims=True)
    dattn_ref[...] = d_attn_gain


def ffn_kernel(
    mn0, mn1, mn2, mn3, cot0, cot1, cot2, cot3, gate_ref, up_ref, down_ref,
    mn_ref, cot_ref, hid_ref, dgate_ref, dup_ref, send_ref, keep_ref,
):
    length = send_ref.shape[1]
    for k, (mn, cot) in enumerate(zip((mn0, mn1, mn2, mn3), (cot0, cot1, cot2, cot3))):
        mn_ref[k * length : (k + 1) * length] = mn[...]
        cot_ref[k * length : (k + 1) * length] = cot[...]

    def half(index, carry):
        rows = block_rows(index, 2 * length)
        gate_pre = dot(mn_ref[rows], gate_ref[...])
        up_pre = dot(mn_ref[rows], up_ref[...])
        d_hidden = dot_t(cot_ref[rows], down_ref[...])
        sig = jax.nn.sigmoid(gate_pre)
        hid_ref[rows] = as_bf(gate_pre * sig * up_pre)
        dgate_ref[rows] = as_bf(d_hidden * up_pre * sig * (1.0 + gate_pre * (1.0 - sig)))
        dup_ref[rows] = as_bf(d_hidden * gate_pre * sig)
        return carry

    lax.fori_loop(0, 2, half, 0)
    emit_partial(
        dot_t(dgate_ref[...], gate_ref[...]) + dot_t(dup_ref[...], up_ref[...]), send_ref, keep_ref
    )


def run_kernel(kernel, outputs, *inputs, scratch=()):
    whole = pl.BlockSpec(memory_space=pltpu.VMEM)
    return pl.pallas_call(
        kernel,
        out_shape=[jax.ShapeDtypeStruct(shape, dtype) for shape, dtype in outputs],
        in_specs=[whole] * len(inputs),
        out_specs=[whole] * len(outputs),
        scratch_shapes=scratch,
        compiler_params=pltpu.CompilerParams(vmem_limit_bytes=48 * 1024 * 1024),
    )(*inputs)


def adamw(weight, grad_sum, mean_old, square_old, step_float, token_total, decay):
    gradient = grad_sum / token_total
    mean_new = BETA_ONE * mean_old + (1.0 - BETA_ONE) * gradient
    square_new = BETA_TWO * square_old + (1.0 - BETA_TWO) * gradient * gradient
    fix_one = 1.0 - jnp.power(BETA_ONE, step_float)
    fix_two = 1.0 - jnp.power(BETA_TWO, step_float)
    change = mean_new / fix_one / (jnp.sqrt(square_new / fix_two) + ADAM_EPS) + decay * weight
    return (weight - LEARN_RATE * change, mean_new, square_new)


def body(
    tokens,
    segments,
    out_cot,
    step_count,
    w_qkv,
    w_out,
    w_gate_up,
    w_down,
    norm_gains,
    mean_qkv,
    mean_out,
    mean_gate_up,
    mean_down,
    mean_gains,
    square_qkv,
    square_out,
    square_gate_up,
    square_down,
    square_gains,
):
    length = tokens.shape[0]
    bf = jnp.bfloat16
    both = ("rep", "shard")
    mine = lax.axis_index("shard")
    own = norm_gains.shape[0]
    extra = jnp.pad(norm_gains.astype(bf)[None], ((0, w_qkv.shape[0] - 1), (0, 128 - own)))
    split, first = split_columns(w_qkv.astype(bf), QKV_WIDTHS, extra)
    turned_out = lax.ppermute(w_out.astype(bf), both, turned(False))
    split_ff, _ = split_columns(w_gate_up.astype(bf), GATE_UP_WIDTHS, ahead=(first,))
    turned_down = lax.ppermute(after(w_down.astype(bf), first), both, turned(False))
    wide, half = QUERY_HEADS * HEAD_SIZE // 4, FF // 4
    whole, steps = gather_rep(
        {
            "q": split[:, :wide],
            "k": split[:, wide:],
            "o": turned_out,
            "g": split_ff[:, :half],
            "u": split_ff[:, half:],
            "d": turned_down,
        }
    )
    w_query, w_keys, output = (whole[n]() for n in "qko")
    gains = w_keys.reshape(-1, w_qkv.shape[0], w_keys.shape[1])
    gains = gains[:, 0, w_keys.shape[1] - 128 : w_keys.shape[1] - 128 + own]
    gains = gains.reshape(1, -1).astype(jnp.float32)
    marks = lax.dynamic_update_slice(jnp.zeros((16, D), bf), segments.astype(bf), (0, 0))
    group = jnp.concatenate([tokens, marks])
    def seen(*events):
        return tuple(steps[event] for event in events if event in steps)

    group = group_gather(after(group, *seen(("q", "z", 1))))
    segment_group = jnp.concatenate([part[length : length + 1, :length] for part in group])
    segment_group = segment_group.astype(jnp.float32)
    attn_gain, mlp_gain = gains[0, :D], gains[0, D : 2 * D]
    cosine, sine = turn_tables(length)
    flat, kv_width = 4 * length, w_keys.shape[1] - 128
    sent = [((2, length, D), bf), ((2, length, D), jnp.float32)]

    x_float = tokens.astype(jnp.float32)
    inv_attn = rms_forward(x_float, attn_gain)[1]
    normed, queries, keys_values, attended_bf, *partial = run_kernel(
        attention_kernel,
        [((flat, D), bf), ((flat, wide), jnp.float32), ((flat, kv_width), jnp.float32), ((flat, wide), bf)]
        + sent,
        *group, segment_group, gains, cosine, sine, w_query, w_keys, output,
    )
    send = after(partial[0], *seen(("g", "z", 2), ("u", "z", 1)))
    cot_group = group_gather(after(out_cot, send))
    x_mid = x_float + group_sum(send, partial[1])
    mid_float, inv_mlp = rms_forward(x_mid, mlp_gain)
    mid_bf = after(mid_float.astype(bf), *seen(("g", "z", 3), ("u", "z", 2)))
    gate, up, down = (whole[n](mid_bf) for n in "gud")
    mid_normed, cot_all, hidden, d_gate, d_up, *partial = run_kernel(
        ffn_kernel,
        [((flat, D), bf), ((flat, D), bf)] + [((flat, half), bf)] * 3 + sent,
        *group_gather(mid_bf),
        *cot_group, gate, up, down,
    )
    rep_down = RepSum(dot(hidden.T, cot_all), True)
    rep_up = RepSum(dot(mid_normed.T, d_up), False)
    rep_gate = RepSum(dot(mid_normed.T, d_gate), False)
    first = rep_down.step(), rep_gate.step(), rep_up.step()
    d_mid_norm = group_sum(*partial)
    d_mid_part, d_mlp_gain = rms_backward(x_mid, inv_mlp, mlp_gain, d_mid_norm)
    d_mid = out_cot.astype(jnp.float32) + d_mid_part
    second = rep_down.step(), rep_gate.step()
    d_mid_bf = jnp.concatenate(group_gather(d_mid.astype(bf)))
    rep_out = RepSum(dot(attended_bf.T, d_mid_bf), False)
    leaving = rep_down.pending(), rep_gate.pending(), rep_up.pending(), rep_out.pending()
    rep_out.step(), rep_down.step(d_mid_bf), rep_gate.step(d_mid_bf), rep_up.step(d_mid_bf)
    d_query, d_keys, d_head_gains, d_attn_gain, *partial = run_kernel(
        attention_back_kernel,
        [((flat, wide), bf), ((flat, kv_width), bf), ((2, HEAD_SIZE), jnp.float32), ((1, D), jnp.float32)]
        + sent,
        after(d_mid_bf, *leaving),
        *group, segment_group, gains, cosine, sine, queries, keys_values, w_query, w_keys, output,
        scratch=[pltpu.VMEM((flat, wide), bf)],
    )

    gain_grads = jnp.concatenate([d_attn_gain[0], d_mlp_gain, d_head_gains.reshape(-1)])
    gain_grads = gain_grads.reshape(-1, 1, 4 * own)
    gain_grads = jnp.pad(gain_grads, ((0, 0), (0, 15), (0, kv_width - 4 * own)))
    grad_keys = dot(normed.T, d_keys).reshape(gain_grads.shape[0], -1, kv_width)
    rep_keys = RepSum(jnp.concatenate([grad_keys, gain_grads], axis=1).reshape(-1, kv_width), True)
    rep_query = RepSum(dot(normed.T, d_query), False)
    begun = rep_keys.step(rep_query.pending()), rep_query.step()
    for _ in range(3):
        rep_keys.step(), rep_query.step()
    for ready in (rep_gate, rep_up, rep_up, rep_out, rep_down, rep_out, rep_out):
        ready.step(begun[0])
    sum_keys, sum_query = rep_keys.total, rep_query.total
    group_rows = grad_keys.shape[1]
    sum_qkv, sum_gain = join_columns(
        jnp.concatenate([sum_query, sum_keys[:group_rows]], axis=1),
        QKV_WIDTHS,
        sum_keys[group_rows, : 4 * own].reshape(4, own),
    )
    d_normed = group_sum(*partial)
    input_grad = d_mid + rms_backward(x_float, inv_attn, attn_gain, d_normed)[0]
    partial = dot(hidden, down).reshape(4, length, D)
    send = after(as_bf(jnp.stack([partial[3], partial[1]])), begun[0])
    layer_out = (x_mid + group_sum(send, (partial[0], partial[2]))).astype(bf)
    sum_gate_up = join_columns(jnp.concatenate([rep_gate.total, rep_up.total], axis=1), GATE_UP_WIDTHS)
    sum_down = lax.ppermute(as_bf(rep_down.total), both, turned(True)).astype(jnp.float32)
    sum_out = lax.ppermute(as_bf(rep_out.total), both, turned(True)).astype(jnp.float32)

    token_total = float(length * lax.axis_size(both))
    step_float = step_count[0].astype(jnp.float32)
    new_qkv, new_mean_qkv, new_square_qkv = adamw(
        w_qkv, sum_qkv, mean_qkv, square_qkv, step_float, token_total, DECAY_RATE
    )
    new_out, new_mean_out, new_square_out = adamw(
        w_out, sum_out, mean_out, square_out, step_float, token_total, DECAY_RATE
    )
    new_gate_up, new_mean_gate_up, new_square_gate_up = adamw(
        w_gate_up, sum_gate_up, mean_gate_up, square_gate_up, step_float, token_total, DECAY_RATE
    )
    new_down, new_mean_down, new_square_down = adamw(
        w_down, sum_down, mean_down, square_down, step_float, token_total, DECAY_RATE
    )
    new_gains, new_mean_gains, new_square_gains = adamw(
        norm_gains, sum_gain, mean_gains, square_gains, step_float, token_total, 0.0
    )
    return (
        layer_out,
        input_grad,
        sum_qkv,
        sum_out,
        sum_gate_up,
        sum_down,
        sum_gain,
        new_qkv,
        new_out,
        new_gate_up,
        new_down,
        new_gains,
        new_mean_qkv,
        new_mean_out,
        new_mean_gate_up,
        new_mean_down,
        new_mean_gains,
        new_square_qkv,
        new_square_out,
        new_square_gate_up,
        new_square_down,
        new_square_gains,
    )


def solution(mesh):
    return jax.shard_map(
        body,
        mesh=mesh,
        in_specs=(
            P(("rep", "shard"), None),
            P(("rep", "shard"), None),
            P(("rep", "shard"), None),
            P(),
            P(("rep", "shard"), None),
            P(("rep", "shard"), None),
            P(("rep", "shard"), None),
            P(("rep", "shard"), None),
            P(("rep", "shard")),
            P(("rep", "shard"), None),
            P(("rep", "shard"), None),
            P(("rep", "shard"), None),
            P(("rep", "shard"), None),
            P(("rep", "shard")),
            P(("rep", "shard"), None),
            P(("rep", "shard"), None),
            P(("rep", "shard"), None),
            P(("rep", "shard"), None),
            P(("rep", "shard")),
        ),
        out_specs=(
            P(("rep", "shard"), None),
            P(("rep", "shard"), None),
            P(("rep", "shard"), None),
            P(("rep", "shard"), None),
            P(("rep", "shard"), None),
            P(("rep", "shard"), None),
            P(("rep", "shard")),
            P(("rep", "shard"), None),
            P(("rep", "shard"), None),
            P(("rep", "shard"), None),
            P(("rep", "shard"), None),
            P(("rep", "shard")),
            P(("rep", "shard"), None),
            P(("rep", "shard"), None),
            P(("rep", "shard"), None),
            P(("rep", "shard"), None),
            P(("rep", "shard")),
            P(("rep", "shard"), None),
            P(("rep", "shard"), None),
            P(("rep", "shard"), None),
            P(("rep", "shard"), None),
            P(("rep", "shard")),
        ),
        check_vma=False,
    )
```
